32 devices in a mesh: seq: 8 (over y, x, core), dp: 4 (over z).
Axes of the slice: x: 2, y: 2, z: 4, core: 2. Of those that a mesh axis runs over, the one named last changes fastest.
Arguments:
- tokens: bfloat16 [4, 1024, 2048], P('dp', 'seq'), may hold values from -6 to 6
- doc_lengths: int32 [4, 8], P('dp'), may hold values from 1 to 512, 1024 in all within a row
- query_weight: bfloat16 [2048, 2048], P(('seq', 'dp')), may hold values from -0.125 to 0.125
- key_weight: bfloat16 [512, 2048], P(('seq', 'dp')), may hold values from -0.125 to 0.125
- value_weight: bfloat16 [512, 2048], P(('seq', 'dp')), may hold values from -0.125 to 0.125
- output_weight: bfloat16 [2048, 2048], P(('seq', 'dp')), may hold values from -1 to 1
- gate_weight: bfloat16 [8192, 2048], P('seq'), may hold values from -0.125 to 0.125
- up_weight: bfloat16 [8192, 2048], P('seq'), may hold values from -0.125 to 0.125
- down_weight: bfloat16 [8192, 2048], P('seq'), may hold values from -0.0625 to 0.0625
- attn_gain: bfloat16 [2048], P(('seq', 'dp')), may hold values from 0.099609375 to 1.8984375
- mlp_gain: bfloat16 [2048], P(('seq', 'dp')), may hold values from 0.099609375 to 1.8984375
- cotangent: bfloat16 [4, 1024, 2048], P('dp', 'seq'), may hold values from -6 to 6
Outputs:
- output: bfloat16 [4, 1024, 2048], P('dp', 'seq')
- grad_tokens: bfloat16 [4, 1024, 2048], P('dp', 'seq')
- grad_query: float32 [2048, 2048], P(('seq', 'dp'))
- grad_key: float32 [512, 2048], P(('seq', 'dp'))
- grad_value: float32 [512, 2048], P(('seq', 'dp'))
- grad_output: float32 [2048, 2048], P(('seq', 'dp'))
- grad_gate: float32 [8192, 2048], P('seq')
- grad_up: float32 [8192, 2048], P('seq')
- grad_down: float32 [8192, 2048], P('seq')
- grad_attn_gain: float32 [2048], P(('seq', 'dp'))
- grad_mlp_gain: float32 [2048], P(('seq', 'dp'))
The draws below stay inside these ranges and needn't reach their ends.
Inputs may be any that keep to these rules, and one draw needn't show every extreme that they name: `doc_lengths`: each sequence's 8 document lengths sum to 1024; its longest document has exactly 512 tokens.
All inputs are finite; a program needn't handle non-finite values.
Results may differ from the reference program's by a relative error of at most 0.015.
Values may be sent and summed in bfloat16 or wider, within the bound.
No kernel may reach another device: no remote copies, remote signals or barrier semaphores. Data moves between devices by JAX's collectives and lax.ppermute only.
A program may use at most 192 MiB of HBM per device.

```python
import math
import jax
import jax.numpy as jnp
import numpy as np
from jax import lax

D = 2048
FF = 8192
HEADS = 32
KV_HEADS = 8
HEAD_DIM = 64
NDOC = 8
QDIM = 2048
KVDIM = 512
SEQ_LEN = 1024
SEQS = 4
N_SEQ = 8


def raised(values, key, source, target, shards_of, factor):
    def block_of(dim):
        return (jnp.arange(values.shape[dim]) // (values.shape[dim] // shards_of)).reshape((-1,) + (1,) * (values.ndim - 1 - dim))

    one_side = jax.random.permutation(key, shards_of)[block_of(target)]
    far = (block_of(target) + shards_of // 2) % shards_of
    return jnp.where((block_of(source) == one_side) | (block_of(source) == far), factor * values, values)


def shard_levels(stream_key, shape, split, least, top_value):
    def one(dim, parts):
        draws = jax.random.uniform(jax.random.fold_in(jax.random.fold_in(stream_key, 6), dim), (parts,), jnp.float32, least / len(split), top_value / len(split))
        return jnp.repeat(jnp.exp(draws), shape[dim] // parts).reshape((-1,) + (1,) * (len(shape) - dim - 1))

    factor_of = one(*split[0])
    for cut in split[1:]:
        factor_of = factor_of * one(*cut)
    return factor_of


def split_up(count, total, most, lean):
    weights = [(1 << 20) // math.isqrt(rank ** lean) + 1 for rank in range(2, count + 1)]
    surplus, counts = total - most - (count - 1), [1] * (count - 1)
    while surplus > 0:
        candidates = [i for i in range(count - 1) if counts[i] < most]
        pool, left = sum([weights[i] for i in candidates]), surplus
        for i in candidates:
            extra = min(most - counts[i], max(1, left * weights[i] // pool), surplus)
            counts[i] = counts[i] + extra
            surplus = surplus - extra
    return np.array([most] + counts)


def ragged(own_key, count, total, reach, lean):
    if count == 2:
        one = jax.random.randint(own_key, (), max(1, total - reach), min(reach, total - 1) + 1)
        return jnp.stack([one, total - one])
    lengths = jnp.asarray(split_up(count, total, reach, lean), jnp.int32)
    twos = (count - 1) // 2
    source_of, sink = lengths[1:1 + 2 * twos:2], lengths[2:2 + 2 * twos:2]
    room = jnp.minimum(source_of - 1, reach - sink)
    moved = jax.random.randint(jax.random.fold_in(own_key, 1), (twos,), 0, 1 << 20) % (room + 1)
    lengths = lengths.at[1:1 + 2 * twos:2].set(source_of - moved).at[2:2 + 2 * twos:2].set(sink + moved)
    return lengths[jax.random.permutation(jax.random.fold_in(own_key, 2), count)]


def bell_draw(stream_key, shape, spread, reach, cuts=(), kind=jnp.bfloat16):
    loudness = shard_levels(stream_key, shape, cuts, -0.22, 0.18) if cuts else 1.0
    values = jax.random.normal(stream_key, shape, jnp.float32) * spread * loudness
    return jnp.minimum(jnp.maximum(values, -reach), reach).astype(kind)


def heavy_noise(key, shape, deviation, limit, pieces, heavy, held_as=jnp.bfloat16):
    values = deviation * jax.random.normal(key, shape, jnp.float32)
    if pieces:
        values = values * shard_levels(key, shape, pieces, -0.22, 0.18)
    return jnp.clip(raised(values, jax.random.fold_in(key, 3), *heavy), -limit, limit).astype(held_as)


def setup_inputs(seed: int = 0) -> dict:
    streams_of = jax.random.split(jax.random.key(seed), 13)
    return {
        "tokens": heavy_noise(streams_of[0], (SEQS, SEQ_LEN, D), 1.0, 6.0, ((0, 4), (1, 8)), (1, 2, 8, 2.0)),
        "doc_lengths": jax.vmap(lambda own: ragged(own, NDOC, SEQ_LEN, SEQ_LEN // 2, 2))(jax.random.split(streams_of[1], SEQS)).reshape((SEQS, NDOC)).astype(jnp.int32),
        "query_weight": bell_draw(streams_of[2], (QDIM, D), D ** -0.5, 0.125, ((0, 32),)),
        "key_weight": bell_draw(streams_of[3], (KVDIM, D), D ** -0.5, 0.125, ((0, 32),)),
        "value_weight": bell_draw(streams_of[4], (KVDIM, D), D ** -0.5, 0.125, ((0, 32),)),
        "output_weight": bell_draw(streams_of[5], (D, QDIM), (QDIM // 64) ** -0.5, 1.0, ((0, 32),)),
        "gate_weight": bell_draw(streams_of[6], (FF, D), D ** -0.5, 0.125, ((0, 8),)),
        "up_weight": bell_draw(streams_of[7], (FF, D), D ** -0.5, 0.125, ((0, 8),)),
        "down_weight": bell_draw(streams_of[8], (FF, D), FF ** -0.5, 0.0625, ((0, 8),)),
        "attn_gain": jnp.clip(1.0 + 0.18 * jax.random.normal(streams_of[9], (D,), jnp.float32), 0.099609375, 1.8984375).astype(jnp.bfloat16),
        "mlp_gain": jnp.clip(1.0 + 0.18 * jax.random.normal(streams_of[10], (D,), jnp.float32), 0.099609375, 1.8984375).astype(jnp.bfloat16),
        "cotangent": heavy_noise(streams_of[11], (SEQS, SEQ_LEN, D), 1.0, 6.0, ((0, 4), (1, 8)), (1, 2, 8, 2.0)),
    }


@jax.custom_vjp
def low(v):
    return lax.optimization_barrier(v.astype(jnp.bfloat16)).astype(jnp.float32)

@jax.custom_vjp
def low_back(v):
    return v

def low_keep(v):
    return (low(v), None)

def low_pass(kept, grad):
    return (grad,)

def back_keep(v):
    return (v, None)

def back_low(kept, grad):
    return (low(grad),)
low.defvjp(low_keep, low_pass)
low_back.defvjp(back_keep, back_low)
norm_eps = 1e-05
highest = lax.Precision.HIGHEST

def by_rows(left, weight_mat):
    return jnp.dot(left, weight_mat.T, precision=highest, preferred_element_type=jnp.float32)

def rms_norm(values, gain_vec):
    return values * lax.rsqrt(lax.optimization_barrier(jnp.mean(values * values, axis=-1, keepdims=True)) + norm_eps) * gain_vec

def rope_tables(positions, head_size):
    half_size = head_size // 2
    exponent = jnp.arange(half_size, dtype=jnp.float32) * 2.0 / head_size
    inverse = 1.0 / 500000.0 ** exponent
    wavelen = 2.0 * math.pi / inverse
    scaled = jnp.where(wavelen > 8192.0, inverse / 32.0, inverse)
    smooth = (8192.0 / wavelen - 1.0) / 3.0
    smoothed = (1.0 - smooth) * scaled / 32.0 + smooth * scaled
    medium = (wavelen >= 2048.0) & (wavelen <= 8192.0)
    inverse = jnp.where(medium, smoothed, scaled)
    angles = positions.astype(jnp.float32)[:, None] * inverse[None, :]
    angles = jnp.concatenate([angles, angles], axis=-1)
    return (jnp.cos(angles), jnp.sin(angles))

def rotate(values, cos_tab, sin_tab):
    half_size = values.shape[-1] // 2
    turned = jnp.concatenate([-values[..., half_size:], values[..., :half_size]], axis=-1)
    return values * cos_tab[:, None, :] + turned * sin_tab[:, None, :]

def doc_layout(doc_lens, total_len):
    doc_ends = jnp.cumsum(doc_lens, dtype=jnp.int32)
    places = jnp.arange(total_len, dtype=jnp.int32)
    passed = (places[:, None] >= doc_ends[None, :]).astype(jnp.int32)
    segment = lax.optimization_barrier(jnp.sum(passed, axis=1, dtype=jnp.int32))
    position = places - lax.optimization_barrier(jnp.sum(passed * doc_lens[None, :], axis=1, dtype=jnp.int32))
    return (segment, position)

def attend(queries, keys_all, values_all, segment):
    total_len = queries.shape[0]
    block_len = min(512, total_len)
    score_scale = HEAD_DIM ** (-0.5)
    key_place = jnp.arange(total_len, dtype=jnp.int32)

    def one_block(begin_at):
        query_blk = lax.dynamic_slice_in_dim(queries, begin_at, block_len, 0)
        row_place = begin_at + jnp.arange(block_len, dtype=jnp.int32)
        seg_blk = lax.dynamic_slice_in_dim(segment, begin_at, block_len, 0)
        raw_scores = low_back(jnp.einsum('qghd,kgd->ghqk', query_blk, keys_all, precision=highest))
        allowed = (key_place[None, :] <= row_place[:, None]) & (segment[None, :] == seg_blk[:, None])
        scores = jnp.where(allowed, raw_scores * score_scale, -1e+30)
        shifted = jnp.exp(scores - lax.optimization_barrier(jnp.max(scores, axis=-1, keepdims=True)))
        soft_probs = low(shifted / lax.optimization_barrier(jnp.sum(shifted, axis=-1, keepdims=True)))
        return low_back(low(jnp.einsum('ghqk,kgd->qghd', soft_probs, values_all, precision=highest)))
    starts = jnp.arange(0, total_len, block_len, dtype=jnp.int32)
    result = lax.map(jax.checkpoint(one_block), starts)
    return result.reshape(total_len, -1)

def layer(tokens_in, query_weight, key_weight, value_weight, output_weight, gate_weight, up_weight, down_weight, attn_gain, mlp_gain, segment, position):
    total_len = tokens_in.shape[0]
    groups = N_SEQ
    per_group = HEADS // N_SEQ
    copies = N_SEQ // KV_HEADS
    normed = low(rms_norm(tokens_in, attn_gain))
    cos_tab, sin_tab = rope_tables(position, HEAD_DIM)
    queries = low_back(by_rows(normed, query_weight)).reshape(total_len, HEADS, HEAD_DIM)
    queries = low_back(low(rotate(queries, cos_tab, sin_tab))).reshape(total_len, groups, per_group, HEAD_DIM)
    keys_lin = low_back(by_rows(normed, key_weight)).reshape(total_len, KV_HEADS, HEAD_DIM)
    keys_all = low_back(jnp.repeat(low(rotate(keys_lin, cos_tab, sin_tab)), copies, axis=1))
    values_lin = low_back(by_rows(normed, value_weight)).reshape(total_len, KV_HEADS, HEAD_DIM)
    values_all = low_back(jnp.repeat(low(values_lin), copies, axis=1))
    mixed = attend(queries, keys_all, values_all, segment)
    hidden_state = tokens_in + low_back(by_rows(mixed, output_weight))
    normed_two = low(rms_norm(hidden_state, mlp_gain))
    gate_val = low_back(by_rows(normed_two, gate_weight))
    up_val = low_back(by_rows(normed_two, up_weight))
    active = low(gate_val / (1.0 + jnp.exp(-gate_val)) * up_val)
    branch_two = low_back(jnp.dot(active, down_weight, precision=highest, preferred_element_type=jnp.float32))
    return hidden_state + branch_two

def reference(tokens, doc_lengths, query_weight, key_weight, value_weight, output_weight, gate_weight, up_weight, down_weight, attn_gain, mlp_gain, cotangent):
    weights = tuple((weight_arr.astype(jnp.float32) for weight_arr in (query_weight, key_weight, value_weight, output_weight, gate_weight, up_weight, down_weight, attn_gain, mlp_gain)))

    def per_sequence(totals, packed):
        seq_tokens, seq_lengths, seq_cot = packed
        segment, position = doc_layout(seq_lengths, SEQ_LEN)

        def forward(tokens_in, *params):
            return layer(tokens_in, *params, segment, position)
        result, pull_back = jax.vjp(forward, seq_tokens.astype(jnp.float32), *weights)
        gradients = pull_back(seq_cot.astype(jnp.float32))
        totals = tuple((before + update for before, update in zip(totals, gradients[1:])))
        return (totals, (result.astype(jnp.bfloat16), gradients[0].astype(jnp.bfloat16)))
    initial = tuple((jnp.zeros(weight_arr.shape, jnp.float32) for weight_arr in weights))
    totals, (outputs, token_grads) = lax.scan(per_sequence, initial, (tokens, doc_lengths, cotangent))
    return (outputs, token_grads, totals[0], totals[1], totals[2], totals[3], totals[4], totals[5], totals[6], totals[7], totals[8])
```

```python
import functools
import math

import jax
import jax.numpy as jnp
from jax import lax
from jax.experimental import pallas as pl
from jax.experimental.pallas import tpu as pltpu
from jax.sharding import PartitionSpec as P

HEADS = 32
KV_HEADS = 8
HEAD_DIM = 64
HALF = HEAD_DIM // 2
NEG = -1e30

norm_eps = 1e-05
bf16 = jnp.bfloat16
f32 = jnp.float32


def by_rows(left, weight_mat):
    return lax.dot_general(
        left, weight_mat, (((1,), (1,)), ((), ())), preferred_element_type=f32
    )


def by_tokens(left, right):
    return lax.dot_general(
        left, right, (((0,), (0,)), ((), ())), preferred_element_type=f32
    )


def plain(left, right):
    return jnp.dot(left, right, preferred_element_type=f32)


def rms_norm(values, gain_vec):
    return (
        values * lax.rsqrt(jnp.mean(values * values, axis=-1, keepdims=True) + norm_eps) * gain_vec
    )


def rope_tables(positions):
    exponent = jnp.arange(HALF, dtype=f32) * 2.0 / HEAD_DIM
    inverse = 1.0 / 500000.0**exponent
    wavelen = 2.0 * math.pi / inverse
    scaled = jnp.where(wavelen > 8192.0, inverse / 32.0, inverse)
    smooth = (8192.0 / wavelen - 1.0) / 3.0
    smoothed = (1.0 - smooth) * scaled / 32.0 + smooth * scaled
    medium = (wavelen >= 2048.0) & (wavelen <= 8192.0)
    inverse = jnp.where(medium, smoothed, scaled)
    angles = positions.astype(f32)[:, None] * inverse[None, :]
    return (jnp.cos(angles), jnp.sin(angles))


def turn(first, second, cos_tab, sin_tab):
    return (first * cos_tab - second * sin_tab, second * cos_tab + first * sin_tab)


def turn_back(first, second, cos_tab, sin_tab):
    return (first * cos_tab + second * sin_tab, second * cos_tab - first * sin_tab)


def gate_grads(d_active, gate_val, up_val, sigmoid_val):
    d_gate = (d_active * up_val * sigmoid_val * (1.0 + gate_val * (1.0 - sigmoid_val))).astype(bf16)
    d_up = (d_active * gate_val * sigmoid_val).astype(bf16)
    return (d_gate, d_up)


def hops(index, count):
    if count == 8:
        return (2, 4) if index % 2 == 0 else (4, 2)
    return tuple(1 << bit for bit in range(1, count.bit_length() - 1))


def half_order(index, count):
    blocks = [index]
    for hop in hops(index, count):
        blocks = blocks + [block ^ hop for block in blocks]
    return blocks


def order_of(index, count):
    return half_order(index, count) + half_order(index ^ 1, count)


def swap(values, count, stage):
    if stage < 0:
        perm = [(i, i ^ 1) for i in range(count)]
    else:
        perm = [(i, i ^ hops(i, count)[stage]) for i in range(count)]
    return lax.ppermute(values, "seq", perm)


def gather_blocks(values, count):
    held = values[None]
    pieces = [values[None]]
    others = []
    for stage in range(len(hops(0, count))):
        arrived = swap(held, count, stage)
        if stage > 0 or len(hops(0, count)) == 1:
            others.append(swap(held if stage == 1 else pieces[-1], count, -1))
        pieces.append(arrived)
        held = jnp.concatenate([held, arrived], axis=0)
    others.append(swap(pieces[-1], count, -1))
    return jnp.concatenate(pieces + others, axis=0)


def scatter_blocks(blocks, count):
    half = count // 2
    total = blocks[:half].astype(f32) + swap(blocks[half:], count, -1).astype(f32)
    for stage in reversed(range(len(hops(0, count)))):
        half = half // 2
        arrived = swap(total[half:].astype(bf16), count, stage)
        total = total[:half] + arrived.astype(f32)
    return total[0]


def ring_gather(values, count):
    pieces = [values]
    for _ in range(count - 1):
        pieces.append(
            lax.ppermute(pieces[-1], "dp", [(i, (i + 1) % count) for i in range(count)])
        )
    return pieces


def in_order(pieces, count):
    stacked = jnp.stack(pieces)
    here = lax.axis_index("dp")
    return jnp.concatenate(
        [
            lax.dynamic_slice_in_dim(stacked, lax.rem(here - i + count, count), 1, 0)
            for i in range(count)
        ]
    )


def ring_scatter(blocks, count):
    here = lax.axis_index("dp")

    def mine(step):
        return lax.dynamic_index_in_dim(
            blocks, lax.rem(here - 1 - step + count, count), 0, keepdims=False
        )

    total = mine(0)
    for step in range(1, count):
        arrived = lax.ppermute(
            total.astype(bf16), "dp", [(i, (i + 1) % count) for i in range(count)]
        )
        total = arrived.astype(f32) + mine(step)
    return total


def sum_everywhere(values, seq_count, dp_count):
    bit = 1
    while bit < dp_count:
        values = values + lax.ppermute(values, "dp", [(i, i ^ bit) for i in range(dp_count)])
        bit *= 2
    bit = 1
    while bit < seq_count:
        values = values + lax.ppermute(values, "seq", [(i, i ^ bit) for i in range(seq_count)])
        bit *= 2
    return values


def picker(width, head, halves):
    lane = lax.broadcasted_iota(jnp.int32, (width, HEAD_DIM), 0)
    part = lax.broadcasted_iota(jnp.int32, (width, HEAD_DIM), 1)
    if halves:
        target = (part // HALF) * (width // 2) + head * HALF + part % HALF
    else:
        target = head * HEAD_DIM + part
    return jnp.where(lane == target, 1.0, 0.0).astype(bf16)


def tile_bias(ends_ref, docs, row_begin, rows, key_begin, keys):
    row = row_begin + lax.broadcasted_iota(jnp.int32, (rows, 1), 0)
    doc_begin = jnp.zeros((rows, 1), jnp.int32)
    for j in range(docs):
        doc_begin = jnp.maximum(doc_begin, jnp.where(row >= ends_ref[j], ends_ref[j], 0))
    key = key_begin + lax.broadcasted_iota(jnp.int32, (rows, keys), 1)
    return jnp.where((key >= doc_begin) & (key <= row), 0.0, NEG)


def row_blocks(total_len):
    rows = min(256, total_len)
    window = total_len // 2
    spans = []
    for begin in range(0, total_len, rows):
        low = max(0, (begin - window + 1) // rows * rows)
        spans.append((begin, low, begin + rows - low))
    return rows, spans


def contract_first(left, right):
    return lax.dot_general(left, right, (((0,), (0,)), ((), ())), preferred_element_type=f32)


def forward_kernel(place_ref, ends_ref, q_ref, k_ref, v_ref, o_ref, log_ref, qs, ks, vs, bias, acc, *, docs, blocks):
    total_len, width = q_ref.shape
    local = total_len // blocks
    for b in range(blocks):
        source = pl.ds(pl.multiple_of(place_ref[b] * local, local), local)
        target = pl.ds(b * local, local)
        qs[target, :] = q_ref[source, :]
        ks[target, :] = k_ref[source, :]
        vs[target, :] = v_ref[source, :]
    rows, spans = row_blocks(total_len)
    for begin, low, keys in spans:
        bias[:, :keys] = tile_bias(ends_ref, docs, begin, rows, low, keys)
        acc[...] = jnp.zeros_like(acc)

        @pl.loop(0, width // HEAD_DIM)
        def _(head):
            q_head = plain(qs[begin : begin + rows, :], picker(width, head, True)).astype(bf16)
            scores = by_rows(q_head, ks[low : low + keys, :]) + bias[:, :keys]
            peak = jnp.max(scores, axis=-1, keepdims=True)
            probs = jnp.exp(scores - peak)
            total = jnp.sum(probs, axis=-1, keepdims=True)
            mixed = plain(probs.astype(bf16), vs[low : low + keys, :]) / total
            acc[...] += by_rows(mixed.astype(bf16), picker(width, head, False))
            log_ref[head, begin : begin + rows, :] = jnp.broadcast_to(
                peak + jnp.log(total), (rows, 128)
            )

        o_ref[begin : begin + rows, :] = acc[...].astype(bf16)


def backward_kernel(
    place_ref, ends_ref, q_ref, k_ref, v_ref, g_ref, log_ref, dq_ref, dk_ref, dv_ref,
    qs, ks, vs, bias, acc, dq, dk, dv, *, docs, blocks,
):
    total_len, width = q_ref.shape
    local = total_len // blocks
    for b in range(blocks):
        source = pl.ds(pl.multiple_of(place_ref[b] * local, local), local)
        target = pl.ds(b * local, local)
        qs[target, :] = q_ref[source, :]
        ks[target, :] = k_ref[source, :]
        vs[target, :] = v_ref[source, :]
    rows, spans = row_blocks(total_len)
    dk[...] = jnp.zeros_like(dk)
    dv[...] = jnp.zeros_like(dv)
    for begin, low, keys in spans:
        bias[:, :keys] = tile_bias(ends_ref, docs, begin, rows, low, keys)
        acc[...] = jnp.zeros_like(acc)

        @pl.loop(0, width // HEAD_DIM)
        def _(head):
            q_pick = picker(width, head, True)
            q_head = plain(qs[begin : begin + rows, :], q_pick).astype(bf16)
            g_head = plain(g_ref[begin : begin + rows, :], picker(width, head, False)).astype(bf16)
            keys_here = ks[low : low + keys, :]
            scores = by_rows(q_head, keys_here) + bias[:, :keys]
            probs = jnp.exp(scores - log_ref[head, begin : begin + rows, 0:1])
            d_probs = by_rows(g_head, vs[low : low + keys, :])
            pushed = probs * d_probs
            delta = jnp.sum(pushed, axis=-1, keepdims=True)
            d_raw = (pushed - probs * delta).astype(bf16)
            d_query = plain(d_raw, keys_here) * (HEAD_DIM ** (-0.5))
            acc[...] += by_rows(d_query.astype(bf16), q_pick)
            dk[low : low + keys, :] += contract_first(d_raw, q_head)
            dv[low : low + keys, :] += contract_first(probs.astype(bf16), g_head)

        dq[begin : begin + rows, :] = acc[...].astype(bf16)
    for b in range(blocks):
        source = pl.ds(b * local, local)
        target = pl.ds(pl.multiple_of(place_ref[b] * local, local), local)
        dq_ref[target, :] = dq[source, :]
        dk_ref[target, :] = dk[source, :].astype(bf16)
        dv_ref[target, :] = dv[source, :].astype(bf16)


def smem():
    return pl.BlockSpec(memory_space=pltpu.SMEM)


def vmem():
    return pl.BlockSpec(memory_space=pltpu.VMEM)


def attend(place, ends, query, key, value, blocks):
    total_len, width = query.shape
    heads = width // HEAD_DIM
    rows, spans = row_blocks(total_len)
    most = max(keys for _, _, keys in spans)
    return pl.pallas_call(
        functools.partial(forward_kernel, docs=ends.shape[0], blocks=blocks),
        out_shape=(
            jax.ShapeDtypeStruct((total_len, width), bf16),
            jax.ShapeDtypeStruct((heads, total_len, 128), f32),
        ),
        in_specs=[smem(), smem(), vmem(), vmem(), vmem()],
        out_specs=(vmem(), vmem()),
        scratch_shapes=[
            pltpu.VMEM((total_len, width), bf16),
            pltpu.VMEM((total_len, HEAD_DIM), bf16),
            pltpu.VMEM((total_len, HEAD_DIM), bf16),
            pltpu.VMEM((rows, most), f32),
            pltpu.VMEM((rows, width), f32),
        ],
        cost_estimate=pl.CostEstimate(
            flops=4 * heads * total_len * total_len * HEAD_DIM,
            bytes_accessed=4 * total_len * width * 2,
            transcendentals=heads * total_len * total_len,
        ),
    )(place, ends, query, key, value)


def attend_back(place, ends, query, key, value, grad, logs, blocks):
    total_len, width = query.shape
    heads = width // HEAD_DIM
    rows, spans = row_blocks(total_len)
    most = max(keys for _, _, keys in spans)
    return pl.pallas_call(
        functools.partial(backward_kernel, docs=ends.shape[0], blocks=blocks),
        out_shape=(
            jax.ShapeDtypeStruct((total_len, width), bf16),
            jax.ShapeDtypeStruct((total_len, HEAD_DIM), bf16),
            jax.ShapeDtypeStruct((total_len, HEAD_DIM), bf16),
        ),
        in_specs=[smem(), smem(), vmem(), vmem(), vmem(), vmem(), vmem()],
        out_specs=(vmem(), vmem(), vmem()),
        scratch_shapes=[
            pltpu.VMEM((total_len, width), bf16),
            pltpu.VMEM((total_len, HEAD_DIM), bf16),
            pltpu.VMEM((total_len, HEAD_DIM), bf16),
            pltpu.VMEM((rows, most), f32),
            pltpu.VMEM((rows, width), f32),
            pltpu.VMEM((total_len, width), bf16),
            pltpu.VMEM((total_len, HEAD_DIM), f32),
            pltpu.VMEM((total_len, HEAD_DIM), f32),
        ],
        cost_estimate=pl.CostEstimate(
            flops=10 * heads * total_len * total_len * HEAD_DIM,
            bytes_accessed=8 * total_len * width * 2,
            transcendentals=heads * total_len * total_len,
        ),
    )(place, ends, query, key, value, grad, logs)


def shards(
    tokens,
    doc_lengths,
    query_weight,
    key_weight,
    value_weight,
    output_weight,
    gate_weight,
    up_weight,
    down_weight,
    attn_gain,
    mlp_gain,
    cotangent,
):
    groups = lax.axis_size("seq")
    dp_count = lax.axis_size("dp")
    my_index = lax.axis_index("seq")
    my_seq = lax.axis_index("dp")
    local_len, width = tokens.shape[1:]
    total_len = local_len * groups
    per_group = HEADS // groups
    copies = groups // KV_HEADS
    group_width = per_group * HEAD_DIM
    gain_rows = attn_gain.shape[0]
    kv_rows = HEAD_DIM // copies
    share = (dp_count - 1) * total_len <= 3 * gate_weight.shape[0]
    my_place = my_index * dp_count + my_seq

    order = jnp.asarray([order_of(i, groups) for i in range(groups)], jnp.int32)[my_index]
    place = jnp.asarray(
        [[order_of(i, groups).index(b) for b in range(groups)] for i in range(groups)], jnp.int32
    )[my_index]

    inputs = tokens[0].astype(f32)
    cot_bf = cotangent[0]

    gains_here = jnp.stack([attn_gain, mlp_gain])
    gains = sum_everywhere(
        lax.dynamic_update_slice(
            jnp.zeros((2, width), bf16), gains_here, (0, my_place * gain_rows)
        ),
        groups,
        dp_count,
    ).astype(f32)
    attn_gain_all, mlp_gain_all = gains[0], gains[1]

    tokens_all = gather_blocks(tokens[0], groups).reshape(total_len, width)
    rows_here = jnp.concatenate([query_weight, key_weight, value_weight], axis=0)
    rows_all = in_order(ring_gather(rows_here, dp_count), dp_count)
    q_rows = query_weight.shape[0]
    k_rows = key_weight.shape[0]
    query_rows = (
        rows_all[:, :q_rows]
        .reshape(per_group, 2, HALF, width)
        .transpose(1, 0, 2, 3)
        .reshape(group_width, width)
    )
    pair_rows = jnp.stack(
        [
            rows_all[:, q_rows : q_rows + k_rows].reshape(kv_rows, width),
            rows_all[:, q_rows + k_rows :].reshape(kv_rows, width),
        ]
    )
    pair_parts = [pair_rows]
    for _ in range(copies.bit_length() - 1):
        step = len(pair_parts)
        arrived = [
            lax.ppermute(part, "seq", [(i, i ^ step) for i in range(groups)]) for part in pair_parts
        ]
        pair_parts = pair_parts + arrived
    if copies > 1:
        stacked = jnp.stack(pair_parts)
        copy_index = lax.rem(my_index, copies)
        pair_rows = jnp.concatenate(
            [
                lax.dynamic_index_in_dim(
                    stacked, jnp.bitwise_xor(copy_index, i), 0, keepdims=False
                )
                for i in range(copies)
            ],
            axis=1,
        )
    key_rows, value_rows = pair_rows[0], pair_rows[1]
    lin_rows = jnp.concatenate([query_rows, key_rows, value_rows], axis=0)

    inputs_all = tokens_all.astype(f32)
    scale_all = lax.rsqrt(jnp.mean(inputs_all * inputs_all, axis=-1, keepdims=True) + norm_eps)
    normed_all = (inputs_all * scale_all * attn_gain_all).astype(bf16)
    lin = by_rows(normed_all, lin_rows)

    ends = jnp.cumsum(doc_lengths[0], dtype=jnp.int32)
    places = (order[:, None] * local_len + jnp.arange(local_len, dtype=jnp.int32)[None]).reshape(-1)
    begins = jnp.max(jnp.where(places[:, None] >= ends[None, :], ends[None, :], 0), axis=1)
    cos_tab, sin_tab = rope_tables(places - begins)
    cos_wide, sin_wide = jnp.tile(cos_tab, (1, per_group)), jnp.tile(sin_tab, (1, per_group))
    half_width = group_width // 2
    score_scale = HEAD_DIM ** (-0.5)
    query = jnp.concatenate(
        turn(lin[:, :half_width], lin[:, half_width:group_width], cos_wide, sin_wide), axis=1
    ).astype(bf16) * jnp.asarray(score_scale, bf16)
    key = jnp.concatenate(
        turn(
            lin[:, group_width : group_width + HALF],
            lin[:, group_width + HALF : group_width + HEAD_DIM],
            cos_tab,
            sin_tab,
        ),
        axis=1,
    ).astype(bf16)
    value = lin[:, group_width + HEAD_DIM :].astype(bf16)

    mixed_heads, logs = attend(place, ends, query, key, value, groups)
    mixed = lax.all_to_all(
        mixed_heads.reshape(groups, local_len, group_width),
        "seq",
        split_axis=0,
        concat_axis=0,
        tiled=True,
    )
    mixed = mixed.transpose(1, 0, 2).reshape(local_len, groups * group_width)

    output_rows = in_order(ring_gather(output_weight, dp_count), dp_count).reshape(-1, HEADS * HEAD_DIM)
    block_width = output_rows.shape[0]
    output_all = gather_blocks(output_rows, groups).reshape(width, HEADS * HEAD_DIM)

    def features_in_order(values):
        return jnp.concatenate(
            [
                lax.dynamic_slice_in_dim(values, place[b] * block_width, block_width, 1)
                for b in range(groups)
            ],
            axis=1,
        )

    def features_by_order(values):
        return jnp.concatenate(
            [
                lax.dynamic_slice_in_dim(values, order[b] * block_width, block_width, 1)
                for b in range(groups)
            ],
            axis=1,
        )

    hidden_state = inputs + features_in_order(by_rows(mixed, output_all))
    normed_two, norm_two_back = jax.vjp(rms_norm, hidden_state, mlp_gain_all)
    normed_two_bf = normed_two.astype(bf16)

    def forward_mlp(normed_toks, cot_toks):
        gate_val = by_rows(normed_toks, gate_weight)
        up_val = by_rows(normed_toks, up_weight)
        sigmoid_val = 1.0 / (1.0 + jnp.exp(-gate_val))
        active = (gate_val * sigmoid_val * up_val).astype(bf16)
        d_active = by_rows(cot_toks, down_weight)
        d_gate, d_up = gate_grads(d_active, gate_val, up_val, sigmoid_val)
        return active, d_gate, d_up

    cot_all = gather_blocks(cot_bf, groups).reshape(total_len, width)
    normed_two_all = gather_blocks(normed_two_bf, groups).reshape(total_len, width)
    active, d_gate, d_up = forward_mlp(normed_two_all, cot_all)
    d_normed_two = scatter_blocks(
        (plain(d_gate, gate_weight) + plain(d_up, up_weight))
        .astype(bf16)
        .reshape(groups, local_len, width),
        groups,
    )
    mlp_out = scatter_blocks(
        plain(active, down_weight).astype(bf16).reshape(groups, local_len, width), groups
    )
    result = (hidden_state + mlp_out).astype(bf16)

    d_hidden_part, grad_mlp_gain = norm_two_back(d_normed_two)
    d_hidden = cot_bf.astype(f32) + d_hidden_part
    d_branch = d_hidden.astype(bf16)
    d_mixed = plain(features_by_order(d_branch), output_all).astype(bf16)
    d_mixed_heads = lax.all_to_all(
        d_mixed.reshape(local_len, groups, group_width).transpose(1, 0, 2),
        "seq",
        split_axis=0,
        concat_axis=0,
        tiled=True,
    ).reshape(total_len, group_width)

    grad_gate = by_tokens(d_gate, normed_two_all)
    grad_up = by_tokens(d_up, normed_two_all)
    grad_down = by_tokens(active, cot_all)
    if share:
        far_cot = jnp.concatenate(ring_gather(cot_bf, dp_count)[1:], axis=0)
        far_normed = jnp.concatenate(ring_gather(normed_two_bf, dp_count)[1:], axis=0)
        far_cot = gather_blocks(far_cot, groups).reshape(-1, width)
        far_normed = gather_blocks(far_normed, groups).reshape(-1, width)
        far_active, far_gate, far_up = forward_mlp(far_normed, far_cot)
        grad_gate = grad_gate + by_tokens(far_gate, far_normed)
        grad_up = grad_up + by_tokens(far_up, far_normed)
        grad_down = grad_down + by_tokens(far_active, far_cot)
    else:
        grad_gate, grad_up, grad_down = (
            lax.psum(grad.astype(bf16), "dp").astype(f32) for grad in (grad_gate, grad_up, grad_down)
        )

    mixed_all = gather_blocks(mixed, groups).reshape(total_len, HEADS * HEAD_DIM)
    d_branch_cols = lax.all_to_all(
        d_branch.reshape(local_len, groups, block_width).transpose(1, 0, 2),
        "seq",
        split_axis=0,
        concat_axis=0,
        tiled=True,
    )
    d_branch_cols = jnp.concatenate(
        [lax.dynamic_slice_in_dim(d_branch_cols, order[b], 1, 0) for b in range(groups)]
    ).reshape(total_len, block_width)
    grad_output = ring_scatter(
        by_tokens(d_branch_cols, mixed_all).reshape(dp_count, -1, HEADS * HEAD_DIM), dp_count
    )

    d_query, d_key, d_value = attend_back(
        place, ends, query, key, value, d_mixed_heads, logs, groups
    )
    if copies > 1:
        d_pair = jnp.stack([d_key, d_value])
        total_pair = d_pair.astype(f32)
        step = 1
        while step < copies:
            total_pair = total_pair + lax.ppermute(
                total_pair, "seq", [(i, i ^ step) for i in range(groups)]
            )
            step *= 2
        d_key, d_value = total_pair[0], total_pair[1]
    d_query, d_key = d_query.astype(f32), d_key.astype(f32)
    d_lin = jnp.concatenate(
        [
            *turn_back(d_query[:, :half_width], d_query[:, half_width:], cos_wide, sin_wide),
            *turn_back(d_key[:, :HALF], d_key[:, HALF:], cos_tab, sin_tab),
            d_value.astype(f32),
        ],
        axis=1,
    ).astype(bf16)
    grad_lin = by_tokens(d_lin, normed_all)
    grad_pair = grad_lin[group_width:].reshape(2, copies, dp_count, -1, width)
    if copies > 1:
        grad_pair = lax.dynamic_index_in_dim(
            grad_pair, lax.rem(my_index, copies), 1, keepdims=True
        )
    grad_rows = jnp.concatenate(
        [
            grad_lin[:group_width]
            .reshape(2, per_group, HALF, width)
            .transpose(1, 0, 2, 3)
            .reshape(dp_count, q_rows, width),
            grad_pair[0, 0],
            grad_pair[1, 0],
        ],
        axis=1,
    )
    grad_rows = ring_scatter(grad_rows, dp_count)

    d_lin_own = d_lin
    if copies > 1:
        lane = jnp.arange(d_lin.shape[1], dtype=jnp.int32)
        keep = (lane < group_width) | (lax.rem(my_index, copies) == 0)
        d_lin_own = jnp.where(keep[None], d_lin, jnp.zeros_like(d_lin))
    d_normed_part = plain(d_lin_own, lin_rows).astype(bf16)
    grad_attn_gain = jnp.sum(d_normed_part.astype(f32) * (inputs_all * scale_all), axis=0)
    d_normed = scatter_blocks(d_normed_part.reshape(groups, local_len, width), groups)
    _, norm_one_back = jax.vjp(lambda v: rms_norm(v, attn_gain_all), inputs)
    d_input = (d_hidden + norm_one_back(d_normed)[0]).astype(bf16)

    gain_grads = sum_everywhere(jnp.stack([grad_attn_gain, grad_mlp_gain]), groups, dp_count)
    gain_grads = lax.dynamic_slice(gain_grads, (0, my_place * gain_rows), (2, gain_rows))

    return (
        result[None],
        d_input[None],
        grad_rows[:q_rows],
        grad_rows[q_rows : q_rows + k_rows],
        grad_rows[q_rows + k_rows :],
        grad_output,
        grad_gate,
        grad_up,
        grad_down,
        gain_grads[0],
        gain_grads[1],
    )


def solution(mesh):
    in_specs = (
        P("dp", "seq", None),
        P("dp", None),
        P(("seq", "dp"), None),
        P(("seq", "dp"), None),
        P(("seq", "dp"), None),
        P(("seq", "dp"), None),
        P("seq", None),
        P("seq", None),
        P("seq", None),
        P(("seq", "dp")),
        P(("seq", "dp")),
        P("dp", "seq", None),
    )
    out_specs = (
        P("dp", "seq", None),
        P("dp", "seq", None),
        P(("seq", "dp"), None),
        P(("seq", "dp"), None),
        P(("seq", "dp"), None),
        P(("seq", "dp"), None),
        P("seq", None),
        P("seq", None),
        P("seq", None),
        P(("seq", "dp")),
        P(("seq", "dp")),
    )
    return jax.shard_map(shards, mesh=mesh, in_specs=in_specs, out_specs=out_specs, check_vma=False)
```

```python
import functools
import math

import jax
import jax.numpy as jnp
from jax import lax
from jax.experimental import pallas as pl
from jax.experimental.pallas import tpu as pltpu
from jax.sharding import PartitionSpec as P

HEADS = 32
KV_HEADS = 8
HEAD_DIM = 64
HALF = HEAD_DIM // 2
NEG = -1e30

norm_eps = 1e-05
bf16 = jnp.bfloat16
f32 = jnp.float32


def by_rows(left, weight_mat):
    return lax.dot_general(
        left, weight_mat, (((1,), (1,)), ((), ())), preferred_element_type=f32
    )


def by_tokens(left, right):
    return lax.dot_general(
        left, right, (((0,), (0,)), ((), ())), preferred_element_type=f32
    )


def plain(left, right):
    return jnp.dot(left, right, preferred_element_type=f32)


def rms_norm(values, gain_vec):
    return (
        values * lax.rsqrt(jnp.mean(values * values, axis=-1, keepdims=True) + norm_eps) * gain_vec
    )


def rope_tables(positions):
    exponent = jnp.arange(HALF, dtype=f32) * 2.0 / HEAD_DIM
    inverse = 1.0 / 500000.0**exponent
    wavelen = 2.0 * math.pi / inverse
    scaled = jnp.where(wavelen > 8192.0, inverse / 32.0, inverse)
    smooth = (8192.0 / wavelen - 1.0) / 3.0
    smoothed = (1.0 - smooth) * scaled / 32.0 + smooth * scaled
    medium = (wavelen >= 2048.0) & (wavelen <= 8192.0)
    inverse = jnp.where(medium, smoothed, scaled)
    angles = positions.astype(f32)[:, None] * inverse[None, :]
    return (jnp.cos(angles), jnp.sin(angles))


def turn(first, second, cos_tab, sin_tab):
    return (first * cos_tab - second * sin_tab, second * cos_tab + first * sin_tab)


def turn_back(first, second, cos_tab, sin_tab):
    return (first * cos_tab + second * sin_tab, second * cos_tab - first * sin_tab)


def hold(values, *others):
    return lax.optimization_barrier((values, *others))[0]


def gate_grads(d_active, gate_val, up_val, sigmoid_val):
    d_gate = (d_active * up_val * sigmoid_val * (1.0 + gate_val * (1.0 - sigmoid_val))).astype(bf16)
    d_up = (d_active * gate_val * sigmoid_val).astype(bf16)
    return (d_gate, d_up)


def hops(index, count):
    if count == 8:
        return (2, 4) if index % 2 == 0 else (4, 2)
    return tuple(1 << bit for bit in range(1, count.bit_length() - 1))


def half_order(index, count):
    blocks = [index]
    for hop in hops(index, count):
        blocks = blocks + [block ^ hop for block in blocks]
    return blocks


def order_of(index, count):
    return half_order(index, count) + half_order(index ^ 1, count)


def swap(values, count, stage):
    if stage < 0:
        perm = [(i, i ^ 1) for i in range(count)]
    else:
        perm = [(i, i ^ hops(i, count)[stage]) for i in range(count)]
    return lax.ppermute(values, "seq", perm)


def gather_pieces(values, count):
    pieces = [values]
    for stage in range(len(hops(0, count))):
        pieces = pieces + [swap(piece, count, stage) for piece in pieces]
    return pieces + [swap(piece, count, -1) for piece in pieces]


def scatter_blocks(mine, theirs, count):
    half = mine.shape[0]
    total = mine.astype(f32) + swap(theirs, count, -1).astype(f32)
    for stage in reversed(range(len(hops(0, count)))):
        half = half // 2
        arrived = swap(total[half:].astype(bf16), count, stage)
        total = total[:half] + arrived.astype(f32)
    return total[0]


def step_on(values, count):
    return lax.ppermute(values, "dp", [(i, (i + 1) % count) for i in range(count)])


def ring_gather(values, count):
    pieces = [values]
    for _ in range(count - 1):
        pieces.append(step_on(pieces[-1], count))
    return pieces


def in_order(pieces, count):
    here = lax.axis_index("dp")
    rows = pieces[0].shape[0]
    whole = jnp.zeros((count * rows, *pieces[0].shape[1:]), pieces[0].dtype)
    for i, piece in enumerate(pieces):
        whole = lax.dynamic_update_slice_in_dim(
            whole, piece, lax.rem(here - i + count, count) * rows, 0
        )
    return whole


def ring_scatter(blocks, count):
    total = blocks[1]
    for step in range(2, count + 1):
        total = step_on(total.astype(bf16), count).astype(f32) + blocks[step % count]
    return total


def sum_everywhere(values, seq_count, dp_count):
    bit = 1
    while bit < dp_count:
        values = values + lax.ppermute(values, "dp", [(i, i ^ bit) for i in range(dp_count)])
        bit *= 2
    bit = 1
    while bit < seq_count:
        values = values + lax.ppermute(values, "seq", [(i, i ^ bit) for i in range(seq_count)])
        bit *= 2
    return values


def smem():
    return pl.BlockSpec(memory_space=pltpu.SMEM)


def vmem():
    return pl.BlockSpec(memory_space=pltpu.VMEM)


def shaped(shape, dtype):
    return jax.ShapeDtypeStruct(shape, dtype)


def call(body, scalars, arrays, outs, scratch, flops, name, **static):
    moved = sum(math.prod(x.shape) * x.dtype.itemsize for x in (*arrays, *outs))
    return pl.pallas_call(
        functools.partial(body, **static),
        out_shape=tuple(outs),
        in_specs=[smem()] * len(scalars) + [vmem()] * len(arrays),
        out_specs=tuple(vmem() for _ in outs),
        scratch_shapes=scratch,
        cost_estimate=pl.CostEstimate(flops=flops, bytes_accessed=moved, transcendentals=0),
        name=name,
    )(*scalars, *arrays)


def picker(width, head, halves):
    lane = lax.broadcasted_iota(jnp.int32, (width, HEAD_DIM), 0)
    part = lax.broadcasted_iota(jnp.int32, (width, HEAD_DIM), 1)
    if halves:
        target = (part // HALF) * (width // 2) + head * HALF + part % HALF
    else:
        target = head * HEAD_DIM + part
    return jnp.where(lane == target, 1.0, 0.0).astype(bf16)


def tile_bias(ends_ref, docs, row_begin, rows, key_begin, keys):
    row = row_begin + lax.broadcasted_iota(jnp.int32, (rows, 1), 0)
    doc_begin = jnp.zeros((rows, 1), jnp.int32)
    for j in range(docs):
        doc_begin = jnp.maximum(doc_begin, jnp.where(row >= ends_ref[j], ends_ref[j], 0))
    key = key_begin + lax.broadcasted_iota(jnp.int32, (rows, keys), 1)
    return jnp.where((key >= doc_begin) & (key <= row), 0.0, NEG)


def row_blocks(total_len):
    rows = min(256, total_len)
    window = total_len // 2
    spans = []
    for begin in range(0, total_len, rows):
        low = max(0, (begin - window + 1) // rows * rows)
        spans.append((begin, low, begin + rows - low))
    return rows, spans


def contract_first(left, right):
    return lax.dot_general(left, right, (((0,), (0,)), ((), ())), preferred_element_type=f32)


def attend_kernel(*refs, docs, blocks, ring, q_rows, k_rows, paired):
    order_ref, ends_ref, dp_ref = refs[:3]
    token_refs = refs[3 : 3 + blocks]
    ring_refs = refs[3 + blocks : 3 + blocks + ring]
    rest = refs[3 + blocks + ring :]
    pair_ref, rest = (rest[0], rest[1:]) if paired else (None, rest)
    gain_ref, cos_ref, sin_ref = rest[:3]
    normed_ref, q_ref, k_ref, v_ref, o_ref, log_ref, lin_rows, bias, acc = rest[3:]
    total_len, width = q_ref.shape
    local = total_len // blocks
    chunk = min(q_rows, HALF)
    for k in range(ring):
        block = lax.rem(dp_ref[0] - k + ring, ring)
        for j in range(q_rows // chunk):
            row = block * q_rows + j * chunk
            target = (
                lax.div(lax.rem(row, HEAD_DIM), HALF) * (width // 2)
                + lax.div(row, HEAD_DIM) * HALF
                + lax.rem(row, HALF)
            )
            lin_rows[pl.ds(pl.multiple_of(target, chunk), chunk), :] = ring_refs[k][
                j * chunk : (j + 1) * chunk, :
            ]
        if not paired:
            for part in range(2):
                target = width + part * HEAD_DIM + block * k_rows
                source = q_rows + part * k_rows
                lin_rows[pl.ds(pl.multiple_of(target, k_rows), k_rows), :] = ring_refs[k][
                    source : source + k_rows, :
                ]
    if paired:
        lin_rows[width:, :] = pair_ref[...]

    few = 32
    for i in range(blocks):

        @pl.loop(0, local // few)
        def _(step, i=i):
            begin = pl.multiple_of(step * few, few)
            values = token_refs[i][pl.ds(begin, few), :].astype(f32)
            scale = lax.rsqrt(jnp.mean(values * values, axis=-1, keepdims=True) + norm_eps)
            normed_ref[pl.ds(pl.multiple_of(i * local + begin, few), few), :] = (
                values * scale * gain_ref[0:1, :]
            ).astype(bf16)

    many = min(256, total_len)

    @pl.loop(0, total_len // many)
    def _(step):
        here = pl.ds(pl.multiple_of(step * many, many), many)
        lin = by_rows(normed_ref[here, :], lin_rows[...])
        cos_tab, sin_tab = cos_ref[here, :], sin_ref[here, :]
        query = jnp.concatenate(
            turn(lin[:, : width // 2], lin[:, width // 2 : width], cos_tab, sin_tab), axis=1
        )
        query = (query * HEAD_DIM ** (-0.5)).astype(bf16)
        key = jnp.concatenate(
            turn(
                lin[:, width : width + HALF],
                lin[:, width + HALF : width + HEAD_DIM],
                cos_tab[:, :HALF],
                sin_tab[:, :HALF],
            ),
            axis=1,
        ).astype(bf16)
        value = lin[:, width + HEAD_DIM :].astype(bf16)
        for j in range(many // local):
            target = pl.ds(
                pl.multiple_of(order_ref[step * (many // local) + j] * local, local), local
            )
            q_ref[target, :] = query[j * local : (j + 1) * local]
            k_ref[target, :] = key[j * local : (j + 1) * local]
            v_ref[target, :] = value[j * local : (j + 1) * local]

    rows, spans = row_blocks(total_len)
    for begin, low, keys in spans:
        bias[:, :keys] = tile_bias(ends_ref, docs, begin, rows, low, keys)
        acc[...] = jnp.zeros_like(acc)

        @pl.loop(0, width // HEAD_DIM)
        def _(head, begin=begin, low=low, keys=keys):
            q_head = plain(q_ref[begin : begin + rows, :], picker(width, head, True)).astype(bf16)
            scores = by_rows(q_head, k_ref[low : low + keys, :]) + bias[:, :keys]
            peak = jnp.max(scores, axis=-1, keepdims=True)
            probs = jnp.exp(scores - peak)
            total = jnp.sum(probs, axis=-1, keepdims=True)
            mixed = plain(probs.astype(bf16), v_ref[low : low + keys, :]) / total
            acc[...] += by_rows(mixed.astype(bf16), picker(width, head, False))
            log_ref[head, begin : begin + rows, :] = jnp.broadcast_to(
                peak + jnp.log(total), (rows, 128)
            )

        o_ref[begin : begin + rows, :] = acc[...].astype(bf16)


def attend(order, ends, here, pieces, ring, pair_rows, gains, cos_wide, sin_wide, group_width, q_rows, k_rows):
    blocks = len(pieces)
    local, width = pieces[0].shape
    total_len = blocks * local
    heads = group_width // HEAD_DIM
    rows, spans = row_blocks(total_len)
    most = max(keys for _, _, keys in spans)
    pair = [] if pair_rows is None else [pair_rows]
    return call(
        attend_kernel,
        (order, ends, here),
        (*pieces, *ring, *pair, gains, cos_wide, sin_wide),
        (
            shaped((total_len, width), bf16),
            shaped((total_len, group_width), bf16),
            shaped((total_len, HEAD_DIM), bf16),
            shaped((total_len, HEAD_DIM), bf16),
            shaped((total_len, group_width), bf16),
            shaped((heads, total_len, 128), f32),
        ),
        [
            pltpu.VMEM((group_width + 2 * HEAD_DIM, width), bf16),
            pltpu.VMEM((rows, most), f32),
            pltpu.VMEM((rows, group_width), f32),
        ],
        2 * total_len * width * (group_width + 128) + 4 * heads * total_len * total_len * HEAD_DIM,
        "attend",
        docs=ends.shape[0],
        blocks=blocks,
        ring=len(ring),
        q_rows=q_rows,
        k_rows=k_rows,
        paired=bool(pair),
    )


def backward_kernel(
    ends_ref, q_ref, k_ref, v_ref, g_ref, log_ref, dq_ref, dk_ref, dv_ref, bias, acc, dk, dv, *, docs
):
    total_len, width = q_ref.shape
    rows, spans = row_blocks(total_len)
    dk[...] = jnp.zeros_like(dk)
    dv[...] = jnp.zeros_like(dv)
    for begin, low, keys in spans:
        bias[:, :keys] = tile_bias(ends_ref, docs, begin, rows, low, keys)
        acc[...] = jnp.zeros_like(acc)

        @pl.loop(0, width // HEAD_DIM)
        def _(head, begin=begin, low=low, keys=keys):
            q_pick = picker(width, head, True)
            q_head = plain(q_ref[begin : begin + rows, :], q_pick).astype(bf16)
            g_head = plain(g_ref[begin : begin + rows, :], picker(width, head, False)).astype(bf16)
            keys_here = k_ref[low : low + keys, :]
            scores = by_rows(q_head, keys_here) + bias[:, :keys]
            probs = jnp.exp(scores - log_ref[head, begin : begin + rows, 0:1])
            d_probs = by_rows(g_head, v_ref[low : low + keys, :])
            pushed = probs * d_probs
            delta = jnp.sum(pushed, axis=-1, keepdims=True)
            d_raw = (pushed - probs * delta).astype(bf16)
            d_query = plain(d_raw, keys_here) * (HEAD_DIM ** (-0.5))
            acc[...] += by_rows(d_query.astype(bf16), q_pick)
            dk[low : low + keys, :] += contract_first(d_raw, q_head)
            dv[low : low + keys, :] += contract_first(probs.astype(bf16), g_head)

        dq_ref[begin : begin + rows, :] = acc[...].astype(bf16)
    dk_ref[...] = dk[...].astype(bf16)
    dv_ref[...] = dv[...].astype(bf16)


def attend_back(ends, query, key, value, grad, logs):
    total_len, width = query.shape
    heads = width // HEAD_DIM
    rows, spans = row_blocks(total_len)
    most = max(keys for _, _, keys in spans)
    return call(
        backward_kernel,
        (ends,),
        (query, key, value, grad, logs),
        (
            shaped((total_len, width), bf16),
            shaped((total_len, HEAD_DIM), bf16),
            shaped((total_len, HEAD_DIM), bf16),
        ),
        [
            pltpu.VMEM((rows, most), f32),
            pltpu.VMEM((rows, width), f32),
            pltpu.VMEM((total_len, HEAD_DIM), f32),
            pltpu.VMEM((total_len, HEAD_DIM), f32),
        ],
        10 * heads * total_len * total_len * HEAD_DIM,
        "attend_back",
        docs=ends.shape[0],
    )


def turn_kernel(order_ref, dq_ref, dk_ref, dv_ref, cos_ref, sin_ref, pick_ref, out_ref, *, blocks):
    total_len, width = dq_ref.shape
    local = total_len // blocks

    @pl.loop(0, blocks)
    def _(i):
        source = pl.ds(pl.multiple_of(order_ref[i] * local, local), local)
        target = pl.ds(pl.multiple_of(i * local, local), local)
        cos_tab, sin_tab = cos_ref[target, :], sin_ref[target, :]
        dq, dk = dq_ref[source, :].astype(f32), dk_ref[source, :].astype(f32)
        turned = jnp.concatenate(
            [
                *turn_back(dq[:, : width // 2], dq[:, width // 2 :], cos_tab, sin_tab),
                *turn_back(dk[:, :HALF], dk[:, HALF:], cos_tab[:, :HALF], sin_tab[:, :HALF]),
                dv_ref[source, :].astype(f32),
            ],
            axis=1,
        ).astype(bf16)
        out_ref[target, :] = plain(turned, pick_ref[...]).astype(bf16)


def project_kernel(order_ref, mixed_ref, token_ref, gain_ref, *refs, blocks):
    weight_refs = refs[:blocks]
    hidden_ref, normed_ref, flat_ref = refs[blocks:]
    local = token_ref.shape[0]
    group_width = mixed_ref.shape[2]
    depth = weight_refs[0].shape[0]
    for g in range(blocks):
        flat_ref[:, g * group_width : (g + 1) * group_width] = mixed_ref[g]
    for i in range(blocks):
        here = pl.ds(pl.multiple_of(order_ref[i] * depth, depth), depth)
        hidden_ref[:, here] = by_rows(flat_ref[...], weight_refs[i][...]) + token_ref[
            :, here
        ].astype(f32)
    few = 32

    @pl.loop(0, local // few)
    def _(step):
        here = pl.ds(pl.multiple_of(step * few, few), few)
        values = hidden_ref[here, :]
        scale = lax.rsqrt(jnp.mean(values * values, axis=-1, keepdims=True) + norm_eps)
        normed_ref[here, :] = (values * scale * gain_ref[1:2, :]).astype(bf16)


def branch_kernel(order_ref, grad_ref, hidden_ref, cot_ref, gain_ref, *refs, blocks):
    weight_refs = refs[:blocks]
    d_hidden_ref, d_mixed_ref, d_branch_ref, gain_out_ref, branch, acc = refs[blocks:]
    local, width = grad_ref.shape
    depth = weight_refs[0].shape[0]
    group_width = d_mixed_ref.shape[2]
    few = 32
    gain_out_ref[...] = jnp.zeros_like(gain_out_ref)

    @pl.loop(0, local // few)
    def _(step):
        here = pl.ds(pl.multiple_of(step * few, few), few)
        values, grads = hidden_ref[here, :], grad_ref[here, :]
        scale = lax.rsqrt(jnp.mean(values * values, axis=-1, keepdims=True) + norm_eps)
        unit = values * scale
        gain_out_ref[0:1, :] += jnp.sum(grads * unit, axis=0, keepdims=True)
        pushed = grads * gain_ref[1:2, :]
        part = scale * (pushed - unit * jnp.mean(pushed * unit, axis=-1, keepdims=True))
        d_hidden = cot_ref[here, :].astype(f32) + part
        d_hidden_ref[here, :] = d_hidden
        branch[here, :] = d_hidden.astype(bf16)

    for i in range(blocks):
        here = pl.ds(pl.multiple_of(order_ref[i] * depth, depth), depth)
        piece = branch[:, here]
        d_branch_ref[order_ref[i]] = piece
        part = plain(piece, weight_refs[i][...])
        if i == 0:
            acc[...] = part
        else:
            acc[...] += part
    for g in range(blocks):
        d_mixed_ref[g] = acc[:, g * group_width : (g + 1) * group_width].astype(bf16)


def outer_kernel(order_ref, grad_ref, *refs, blocks):
    mixed_refs, out_ref = refs[:blocks], refs[blocks]
    for i in range(blocks):
        part = contract_first(grad_ref[order_ref[i]], mixed_refs[i][...])
        if i == 0:
            out_ref[...] = part
        else:
            out_ref[...] += part


def shards(
    tokens,
    doc_lengths,
    query_weight,
    key_weight,
    value_weight,
    output_weight,
    gate_weight,
    up_weight,
    down_weight,
    attn_gain,
    mlp_gain,
    cotangent,
):
    groups = lax.axis_size("seq")
    dp_count = lax.axis_size("dp")
    my_index = lax.axis_index("seq")
    my_seq = lax.axis_index("dp")
    local_len, width = tokens.shape[1:]
    total_len = local_len * groups
    per_group = HEADS // groups
    copies = groups // KV_HEADS
    group_width = per_group * HEAD_DIM
    all_heads = HEADS * HEAD_DIM
    gain_rows = attn_gain.shape[0]
    kv_rows = HEAD_DIM // copies
    q_rows, k_rows = query_weight.shape[0], key_weight.shape[0]
    ring_rows = q_rows + 2 * k_rows
    half = groups // 2
    share = (dp_count - 1) * total_len <= 3 * gate_weight.shape[0]
    my_place = my_index * dp_count + my_seq

    order = jnp.asarray([order_of(i, groups) for i in range(groups)], jnp.int32)[my_index]
    here = my_seq.reshape(1).astype(jnp.int32)
    token_bf, cot_bf = tokens[0], cotangent[0]

    rows_here = jnp.concatenate([query_weight, key_weight, value_weight], axis=0)
    ring = ring_gather(rows_here, dp_count)
    token_pieces = gather_pieces(token_bf, groups)
    gains = sum_everywhere(
        lax.dynamic_update_slice(
            jnp.zeros((2, width), bf16),
            jnp.stack([attn_gain, mlp_gain]),
            (0, my_place * gain_rows),
        ),
        groups,
        dp_count,
    ).astype(f32)
    pair_rows = None
    copy_index = lax.rem(my_index, copies)
    if copies > 1:
        in_ring = in_order(ring, dp_count).reshape(dp_count, ring_rows, width)
        own = jnp.stack(
            [
                in_ring[:, q_rows : q_rows + k_rows].reshape(kv_rows, width),
                in_ring[:, q_rows + k_rows :].reshape(kv_rows, width),
            ]
        )
        parts = [own]
        for bit in range(copies.bit_length() - 1):
            parts = parts + [
                lax.ppermute(part, "seq", [(i, i ^ (1 << bit)) for i in range(groups)])
                for part in parts
            ]
        stacked = jnp.stack(parts)
        pair_rows = jnp.concatenate(
            [
                lax.dynamic_index_in_dim(
                    stacked, jnp.bitwise_xor(copy_index, i), 0, keepdims=False
                )
                for i in range(copies)
            ],
            axis=1,
        ).reshape(2 * HEAD_DIM, width)

    ends = jnp.cumsum(doc_lengths[0], dtype=jnp.int32)
    places = (order[:, None] * local_len + jnp.arange(local_len, dtype=jnp.int32)[None]).reshape(-1)
    begins = jnp.max(jnp.where(places[:, None] >= ends[None, :], ends[None, :], 0), axis=1)
    cos_tab, sin_tab = rope_tables(places - begins)
    cos_wide, sin_wide = jnp.tile(cos_tab, (1, per_group)), jnp.tile(sin_tab, (1, per_group))

    normed_all, query, key, value, mixed_heads, logs = attend(
        order, ends, here, token_pieces, ring, pair_rows, gains, cos_wide, sin_wide,
        group_width, q_rows, k_rows,
    )
    mixed = lax.all_to_all(
        mixed_heads.reshape(groups, local_len, group_width),
        "seq",
        split_axis=0,
        concat_axis=0,
        tiled=True,
    )

    cot_pieces = gather_pieces(hold(cot_bf, token_pieces[1], token_pieces[2]), groups)

    output_ring = ring_gather(hold(output_weight, ring[-1]), dp_count)
    output_rows = in_order(output_ring, dp_count)
    output_pieces = gather_pieces(hold(output_rows, cot_pieces[1], cot_pieces[2]), groups)

    hidden_state, normed_two, mixed_flat = call(
        project_kernel,
        (order,),
        (mixed, token_bf, gains, *output_pieces),
        (
            shaped((local_len, width), f32),
            shaped((local_len, width), bf16),
            shaped((local_len, all_heads), bf16),
        ),
        [],
        2 * local_len * width * all_heads,
        "project",
        blocks=groups,
    )
    normed_two_pieces = gather_pieces(normed_two, groups)
    follow = (normed_two_pieces[1], normed_two_pieces[2])
    if share:
        cot_ring = ring_gather(hold(cot_bf, output_ring[-1]), dp_count)[1:]
        far_cot_pieces = gather_pieces(hold(jnp.concatenate(cot_ring, axis=0), *follow), groups)
        follow = (far_cot_pieces[1], far_cot_pieces[2])
    mixed_pieces = gather_pieces(hold(mixed_flat, *follow), groups)
    follow = (mixed_pieces[1], mixed_pieces[2])
    if share:
        normed_ring = ring_gather(normed_two, dp_count)[1:]
        far_normed_pieces = gather_pieces(
            hold(jnp.concatenate(normed_ring, axis=0), *follow), groups
        )

    def forward_mlp(normed_toks, cot_toks):
        gate_val = by_rows(normed_toks, gate_weight)
        up_val = by_rows(normed_toks, up_weight)
        sigmoid_val = 1.0 / (1.0 + jnp.exp(-gate_val))
        active = (gate_val * sigmoid_val * up_val).astype(bf16)
        d_active = by_rows(cot_toks, down_weight)
        d_gate, d_up = gate_grads(d_active, gate_val, up_val, sigmoid_val)
        return active, d_gate, d_up

    cot_all = jnp.concatenate(cot_pieces, axis=0)
    normed_two_all = jnp.concatenate(normed_two_pieces, axis=0)
    active, d_gate, d_up = forward_mlp(normed_two_all, cot_all)
    d_blocks = (
        (plain(d_gate, gate_weight) + plain(d_up, up_weight))
        .astype(bf16)
        .reshape(groups, local_len, width)
    )
    if share:
        d_blocks = hold(d_blocks, normed_ring[-1])
    d_normed_two = scatter_blocks(d_blocks[:half], d_blocks[half:], groups)
    mlp_blocks = hold(
        plain(active, down_weight).astype(bf16).reshape(groups, local_len, width), d_normed_two
    )
    mlp_out = scatter_blocks(mlp_blocks[:half], mlp_blocks[half:], groups)
    result = (hidden_state + mlp_out).astype(bf16)

    d_hidden, d_mixed, d_branch, grad_mlp_gain = call(
        branch_kernel,
        (order,),
        (d_normed_two, hidden_state, cot_bf, gains, *output_pieces),
        (
            shaped((local_len, width), f32),
            shaped((groups, local_len, group_width), bf16),
            shaped((groups, local_len, output_rows.shape[0]), bf16),
            shaped((1, width), f32),
        ),
        [pltpu.VMEM((local_len, width), bf16), pltpu.VMEM((local_len, all_heads), f32)],
        2 * local_len * width * all_heads,
        "branch",
        blocks=groups,
    )
    d_mixed_heads = lax.all_to_all(
        d_mixed, "seq", split_axis=0, concat_axis=0, tiled=True
    ).reshape(total_len, group_width)
    d_branch_cols = lax.all_to_all(d_branch, "seq", split_axis=0, concat_axis=0, tiled=True)

    grad_gate = by_tokens(d_gate, normed_two_all)
    grad_up = by_tokens(d_up, normed_two_all)
    grad_down = by_tokens(active, cot_all)
    if share:
        far_cot = jnp.concatenate(far_cot_pieces, axis=0)
        far_normed = jnp.concatenate(far_normed_pieces, axis=0)
        far_active, far_gate, far_up = forward_mlp(far_normed, far_cot)
        grad_gate = grad_gate + by_tokens(far_gate, far_normed)
        grad_up = grad_up + by_tokens(far_up, far_normed)
        grad_down = grad_down + by_tokens(far_active, far_cot)
        d_mixed_heads = hold(d_mixed_heads, far_normed_pieces[3], mixed_pieces[3])
    else:
        grad_gate, grad_up, grad_down = (
            lax.psum(grad.astype(bf16), "dp").astype(f32) for grad in (grad_gate, grad_up, grad_down)
        )

    grad_output = call(
        outer_kernel,
        (order,),
        (d_branch_cols, *mixed_pieces),
        (shaped((output_rows.shape[0], all_heads), f32),),
        [],
        2 * total_len * output_rows.shape[0] * all_heads,
        "outer",
        blocks=groups,
    )[0].reshape(dp_count, -1, all_heads)
    grad_output = ring_scatter(
        [
            lax.dynamic_index_in_dim(
                grad_output, lax.rem(my_seq - k + dp_count, dp_count), 0, keepdims=False
            )
            for k in range(dp_count)
        ],
        dp_count,
    )

    d_query, d_key, d_value = attend_back(ends, query, key, value, d_mixed_heads, logs)
    if copies > 1:
        total_pair = jnp.stack([d_key, d_value]).astype(f32)
        for bit in range(copies.bit_length() - 1):
            total_pair = total_pair + lax.ppermute(
                total_pair, "seq", [(i, i ^ (1 << bit)) for i in range(groups)]
            )
        d_key, d_value = total_pair[0], total_pair[1]

    column = jnp.arange(dp_count * ring_rows, dtype=jnp.int32)
    block = lax.rem(my_seq - column // ring_rows + dp_count, dp_count)
    within = column % ring_rows
    row = block * q_rows + within
    from_query = (
        (row % HEAD_DIM) // HALF * (group_width // 2) + row // HEAD_DIM * HALF + row % HALF
    )
    pair = (within - q_rows) // k_rows
    from_pair = (
        group_width
        + pair * HEAD_DIM
        + copy_index * kv_rows
        + block * k_rows
        + (within - q_rows) % k_rows
    )
    source = jnp.where(within < q_rows, from_query, from_pair)
    pick = (
        jnp.arange(group_width + 2 * HEAD_DIM, dtype=jnp.int32)[:, None] == source[None, :]
    ).astype(bf16)
    d_lin = call(
        turn_kernel,
        (order,),
        (d_query, d_key, d_value, cos_wide, sin_wide, pick),
        (shaped((total_len, dp_count * ring_rows), bf16),),
        [],
        2 * total_len * dp_count * ring_rows * (group_width + 2 * HEAD_DIM),
        "turn",
        blocks=groups,
    )[0]
    grad_rows = ring_scatter(
        list(by_tokens(d_lin, normed_all).reshape(dp_count, ring_rows, width)), dp_count
    )

    inputs_all = jnp.concatenate(token_pieces, axis=0).astype(f32)
    scale_all = lax.rsqrt(jnp.mean(inputs_all * inputs_all, axis=-1, keepdims=True) + norm_eps)
    d_normed_part = plain(d_lin, jnp.concatenate(ring, axis=0)).astype(bf16)
    grad_attn_gain = jnp.sum(d_normed_part.astype(f32) * (inputs_all * scale_all), axis=0)
    d_normed_part = d_normed_part.reshape(groups, local_len, width)
    d_normed = scatter_blocks(d_normed_part[:half], d_normed_part[half:], groups)
    inputs = token_bf.astype(f32)
    _, norm_one_back = jax.vjp(lambda v: rms_norm(v, gains[0]), inputs)
    d_input = (d_hidden + norm_one_back(d_normed)[0]).astype(bf16)

    gain_grads = sum_everywhere(
        jnp.stack([grad_attn_gain, grad_mlp_gain[0]]), groups, dp_count
    )
    gain_grads = lax.dynamic_slice(gain_grads, (0, my_place * gain_rows), (2, gain_rows))

    return (
        result[None],
        d_input[None],
        grad_rows[:q_rows],
        grad_rows[q_rows : q_rows + k_rows],
        grad_rows[q_rows + k_rows :],
        grad_output,
        grad_gate,
        grad_up,
        grad_down,
        gain_grads[0],
        gain_grads[1],
    )


def solution(mesh):
    in_specs = (
        P("dp", "seq", None),
        P("dp", None),
        P(("seq", "dp"), None),
        P(("seq", "dp"), None),
        P(("seq", "dp"), None),
        P(("seq", "dp"), None),
        P("seq", None),
        P("seq", None),
        P("seq", None),
        P(("seq", "dp")),
        P(("seq", "dp")),
        P("dp", "seq", None),
    )
    out_specs = (
        P("dp", "seq", None),
        P("dp", "seq", None),
        P(("seq", "dp"), None),
        P(("seq", "dp"), None),
        P(("seq", "dp"), None),
        P(("seq", "dp"), None),
        P("seq", None),
        P("seq", None),
        P("seq", None),
        P(("seq", "dp")),
        P(("seq", "dp")),
    )
    return jax.shard_map(shards, mesh=mesh, in_specs=in_specs, out_specs=out_specs, check_vma=False)
```

```python
import functools
import math

import jax
import jax.numpy as jnp
from jax import lax
from jax.experimental import pallas as pl
from jax.experimental.pallas import tpu as pltpu
from jax.sharding import PartitionSpec as P

HEADS = 32
KV_HEADS = 8
HEAD_DIM = 64
HALF = HEAD_DIM // 2
NEG = -1e30

norm_eps = 1e-05
bf16 = jnp.bfloat16
f32 = jnp.float32


def by_rows(left, weight_mat):
    return lax.dot_general(
        left, weight_mat, (((1,), (1,)), ((), ())), preferred_element_type=f32
    )


def by_tokens(left, right):
    return lax.dot_general(
        left, right, (((0,), (0,)), ((), ())), preferred_element_type=f32
    )


def plain(left, right):
    return jnp.dot(left, right, preferred_element_type=f32)


def rms_norm(values, gain_vec):
    return (
        values * lax.rsqrt(jnp.mean(values * values, axis=-1, keepdims=True) + norm_eps) * gain_vec
    )


def rope_tables(positions):
    exponent = jnp.arange(HALF, dtype=f32) * 2.0 / HEAD_DIM
    inverse = 1.0 / 500000.0**exponent
    wavelen = 2.0 * math.pi / inverse
    scaled = jnp.where(wavelen > 8192.0, inverse / 32.0, inverse)
    smooth = (8192.0 / wavelen - 1.0) / 3.0
    smoothed = (1.0 - smooth) * scaled / 32.0 + smooth * scaled
    medium = (wavelen >= 2048.0) & (wavelen <= 8192.0)
    inverse = jnp.where(medium, smoothed, scaled)
    angles = positions.astype(f32)[:, None] * inverse[None, :]
    return (jnp.cos(angles), jnp.sin(angles))


def turn(first, second, cos_tab, sin_tab):
    return (first * cos_tab - second * sin_tab, second * cos_tab + first * sin_tab)


def turn_back(first, second, cos_tab, sin_tab):
    return (first * cos_tab + second * sin_tab, second * cos_tab - first * sin_tab)


def hold(values, *others):
    return lax.optimization_barrier((values, *others))[0]


def gate_grads(d_active, gate_val, up_val, sigmoid_val):
    d_gate = (d_active * up_val * sigmoid_val * (1.0 + gate_val * (1.0 - sigmoid_val))).astype(bf16)
    d_up = (d_active * gate_val * sigmoid_val).astype(bf16)
    return (d_gate, d_up)


def hops(index, count):
    if count == 8:
        return (2, 4) if index % 2 == 0 else (4, 2)
    return tuple(1 << bit for bit in range(1, count.bit_length() - 1))


def half_order(index, count):
    blocks = [index]
    for hop in hops(index, count):
        blocks = blocks + [block ^ hop for block in blocks]
    return blocks


def order_of(index, count):
    return half_order(index, count) + half_order(index ^ 1, count)


def swap(values, count, stage):
    if stage < 0:
        perm = [(i, i ^ 1) for i in range(count)]
    else:
        perm = [(i, i ^ hops(i, count)[stage]) for i in range(count)]
    return lax.ppermute(values, "seq", perm)


def gather_pieces(values, count):
    pieces = [values]
    for stage in range(len(hops(0, count))):
        pieces = pieces + [swap(piece, count, stage) for piece in pieces]
    return pieces + [swap(piece, count, -1) for piece in pieces]


def scatter_blocks(mine, theirs, count):
    half = mine.shape[0]
    total = mine.astype(f32) + swap(theirs, count, -1).astype(f32)
    for stage in reversed(range(len(hops(0, count)))):
        half = half // 2
        arrived = swap(total[half:].astype(bf16), count, stage)
        total = total[:half] + arrived.astype(f32)
    return total[0]


def scatter_steps(mine, theirs, count):
    half = mine.shape[0]
    arrived = swap(theirs, count, -1)
    total = mine.astype(f32)
    for stage in reversed(range(len(hops(0, count)))):
        after = yield theirs
        total = total + (arrived if after is None else hold(arrived, after)).astype(f32)
        half = half // 2
        theirs = total[half:].astype(bf16)
        total = total[:half]
        arrived = swap(theirs, count, stage)
    after = yield theirs
    total = total + (arrived if after is None else hold(arrived, after)).astype(f32)
    yield total[0]


def run_steps(steps):
    last = None
    for last in steps:
        pass
    return last


def across(values, count, k):
    return lax.ppermute(values, "dp", [(i, i ^ k) for i in range(count)])


def far_gather(values, count):
    return [values] + [across(values, count, k) for k in range(1, count)]


def in_order(pieces, count):
    here = lax.axis_index("dp")
    rows = pieces[0].shape[0]
    whole = jnp.zeros((count * rows, *pieces[0].shape[1:]), pieces[0].dtype)
    for k, piece in enumerate(pieces):
        whole = lax.dynamic_update_slice_in_dim(whole, piece, jnp.bitwise_xor(here, k) * rows, 0)
    return whole


def far_send(blocks, count):
    return [blocks[0]] + [across(blocks[k].astype(bf16), count, k) for k in range(1, count)]


def far_sum(parts):
    total = parts[0]
    for part in parts[1:]:
        total = total + part.astype(f32)
    return total


def sum_steps(values, seq_count, dp_count):
    moves = [("dp", dp_count, 1 << b) for b in range(dp_count.bit_length() - 1)]
    moves += [("seq", seq_count, 1 << b) for b in range(seq_count.bit_length() - 1)]
    for axis, count, bit in moves:
        arrived = lax.ppermute(values, axis, [(i, i ^ bit) for i in range(count)])
        after = yield values
        values = values + (arrived if after is None else hold(arrived, after))
    yield values


def sum_everywhere(values, seq_count, dp_count):
    return run_steps(sum_steps(values, seq_count, dp_count))


def smem():
    return pl.BlockSpec(memory_space=pltpu.SMEM)


def vmem():
    return pl.BlockSpec(memory_space=pltpu.VMEM)


def shaped(shape, dtype):
    return jax.ShapeDtypeStruct(shape, dtype)


def call(body, scalars, arrays, outs, scratch, flops, name, **static):
    moved = sum(math.prod(x.shape) * x.dtype.itemsize for x in (*arrays, *outs))
    return pl.pallas_call(
        functools.partial(body, **static),
        out_shape=tuple(outs),
        in_specs=[smem()] * len(scalars) + [vmem()] * len(arrays),
        out_specs=tuple(vmem() for _ in outs),
        scratch_shapes=scratch,
        cost_estimate=pl.CostEstimate(flops=flops, bytes_accessed=moved, transcendentals=0),
        name=name,
    )(*scalars, *arrays)


def picker(width, head, halves):
    lane = lax.broadcasted_iota(jnp.int32, (width, HEAD_DIM), 0)
    part = lax.broadcasted_iota(jnp.int32, (width, HEAD_DIM), 1)
    if halves:
        target = (part // HALF) * (width // 2) + head * HALF + part % HALF
    else:
        target = head * HEAD_DIM + part
    return jnp.where(lane == target, 1.0, 0.0).astype(bf16)


def tile_bias(ends_ref, docs, row_begin, rows, key_begin, keys):
    row = row_begin + lax.broadcasted_iota(jnp.int32, (rows, 1), 0)
    doc_begin = jnp.zeros((rows, 1), jnp.int32)
    for j in range(docs):
        doc_begin = jnp.maximum(doc_begin, jnp.where(row >= ends_ref[j], ends_ref[j], 0))
    key = key_begin + lax.broadcasted_iota(jnp.int32, (rows, keys), 1)
    return jnp.where((key >= doc_begin) & (key <= row), 0.0, NEG)


def row_blocks(total_len):
    rows = min(256, total_len)
    window = total_len // 2
    spans = []
    for begin in range(0, total_len, rows):
        low = max(0, (begin - window + 1) // rows * rows)
        spans.append((begin, low, begin + rows - low))
    return rows, spans


def contract_first(left, right):
    return lax.dot_general(left, right, (((0,), (0,)), ((), ())), preferred_element_type=f32)


def input_kernel(*refs, blocks, ring, q_rows, k_rows, paired):
    order_ref, dp_ref = refs[:2]
    token_refs = refs[2 : 2 + blocks]
    ring_refs = refs[2 + blocks : 2 + blocks + ring]
    rest = refs[2 + blocks + ring :]
    pair_ref, rest = (rest[0], rest[1:]) if paired else (None, rest)
    gain_ref, cos_ref, sin_ref = rest[:3]
    normed_ref, q_ref, k_ref, v_ref, lin_rows = rest[3:]
    total_len, width = q_ref.shape
    local = total_len // blocks
    chunk = min(q_rows, HALF)
    for k in range(ring):
        block = jnp.bitwise_xor(dp_ref[0], k)
        for j in range(q_rows // chunk):
            row = block * q_rows + j * chunk
            target = (
                lax.div(lax.rem(row, HEAD_DIM), HALF) * (width // 2)
                + lax.div(row, HEAD_DIM) * HALF
                + lax.rem(row, HALF)
            )
            lin_rows[pl.ds(pl.multiple_of(target, chunk), chunk), :] = ring_refs[k][
                j * chunk : (j + 1) * chunk, :
            ]
        if not paired:
            for part in range(2):
                target = width + part * HEAD_DIM + block * k_rows
                source = q_rows + part * k_rows
                lin_rows[pl.ds(pl.multiple_of(target, k_rows), k_rows), :] = ring_refs[k][
                    source : source + k_rows, :
                ]
    if paired:
        lin_rows[width:, :] = pair_ref[...]

    few = 32
    for i in range(blocks):

        @pl.loop(0, local // few)
        def _(step, i=i):
            begin = pl.multiple_of(step * few, few)
            values = token_refs[i][pl.ds(begin, few), :].astype(f32)
            scale = lax.rsqrt(jnp.mean(values * values, axis=-1, keepdims=True) + norm_eps)
            normed_ref[pl.ds(pl.multiple_of(i * local + begin, few), few), :] = (
                values * scale * gain_ref[0:1, :]
            ).astype(bf16)

    many = min(256, total_len)

    @pl.loop(0, total_len // many)
    def _(step):
        here = pl.ds(pl.multiple_of(step * many, many), many)
        lin = by_rows(normed_ref[here, :], lin_rows[...])
        cos_tab, sin_tab = cos_ref[here, :], sin_ref[here, :]
        query = jnp.concatenate(
            turn(lin[:, : width // 2], lin[:, width // 2 : width], cos_tab, sin_tab), axis=1
        )
        query = (query * HEAD_DIM ** (-0.5)).astype(bf16)
        key = jnp.concatenate(
            turn(
                lin[:, width : width + HALF],
                lin[:, width + HALF : width + HEAD_DIM],
                cos_tab[:, :HALF],
                sin_tab[:, :HALF],
            ),
            axis=1,
        ).astype(bf16)
        value = lin[:, width + HEAD_DIM :].astype(bf16)
        for j in range(many // local):
            target = pl.ds(
                pl.multiple_of(order_ref[step * (many // local) + j] * local, local), local
            )
            q_ref[target, :] = query[j * local : (j + 1) * local]
            k_ref[target, :] = key[j * local : (j + 1) * local]
            v_ref[target, :] = value[j * local : (j + 1) * local]


def attend_kernel(ends_ref, q_ref, k_ref, v_ref, o_ref, log_ref, bias, acc, *, docs):
    total_len, width = q_ref.shape
    rows, spans = row_blocks(total_len)
    for begin, low, keys in spans:
        bias[:, :keys] = tile_bias(ends_ref, docs, begin, rows, low, keys)
        acc[...] = jnp.zeros_like(acc)

        @pl.loop(0, width // HEAD_DIM)
        def _(head, begin=begin, low=low, keys=keys):
            q_head = plain(q_ref[begin : begin + rows, :], picker(width, head, True)).astype(bf16)
            scores = by_rows(q_head, k_ref[low : low + keys, :]) + bias[:, :keys]
            peak = jnp.max(scores, axis=-1, keepdims=True)
            probs = jnp.exp(scores - peak)
            total = jnp.sum(probs, axis=-1, keepdims=True)
            mixed = plain(probs.astype(bf16), v_ref[low : low + keys, :]) / total
            acc[...] += by_rows(mixed.astype(bf16), picker(width, head, False))
            log_ref[head, begin : begin + rows, :] = jnp.broadcast_to(
                peak + jnp.log(total), (rows, 128)
            )

        o_ref[begin : begin + rows, :] = acc[...].astype(bf16)


def project_in(order, here, pieces, ring, pair_rows, gains, cos_wide, sin_wide, group_width, q_rows, k_rows):
    blocks = len(pieces)
    local, width = pieces[0].shape
    total_len = blocks * local
    pair = [] if pair_rows is None else [pair_rows]
    return call(
        input_kernel,
        (order, here),
        (*pieces, *ring, *pair, gains, cos_wide, sin_wide),
        (
            shaped((total_len, width), bf16),
            shaped((total_len, group_width), bf16),
            shaped((total_len, HEAD_DIM), bf16),
            shaped((total_len, HEAD_DIM), bf16),
        ),
        [pltpu.VMEM((group_width + 2 * HEAD_DIM, width), bf16)],
        2 * total_len * width * (group_width + 128),
        "project_in",
        blocks=blocks,
        ring=len(ring),
        q_rows=q_rows,
        k_rows=k_rows,
        paired=bool(pair),
    )


def attend(ends, query, key, value):
    total_len, group_width = query.shape
    heads = group_width // HEAD_DIM
    rows, spans = row_blocks(total_len)
    most = max(keys for _, _, keys in spans)
    return call(
        attend_kernel,
        (ends,),
        (query, key, value),
        (shaped((total_len, group_width), bf16), shaped((heads, total_len, 128), f32)),
        [pltpu.VMEM((rows, most), f32), pltpu.VMEM((rows, group_width), f32)],
        8 * heads * total_len * total_len * HEAD_DIM,
        "attend",
        docs=ends.shape[0],
    )


def backward_kernel(
    ends_ref, q_ref, k_ref, v_ref, g_ref, log_ref, dq_ref, dk_ref, dv_ref, bias, acc, dk, dv, *, docs
):
    total_len, width = q_ref.shape
    rows, spans = row_blocks(total_len)
    dk[...] = jnp.zeros_like(dk)
    dv[...] = jnp.zeros_like(dv)
    for begin, low, keys in spans:
        bias[:, :keys] = tile_bias(ends_ref, docs, begin, rows, low, keys)
        acc[...] = jnp.zeros_like(acc)

        @pl.loop(0, width // HEAD_DIM)
        def _(head, begin=begin, low=low, keys=keys):
            q_pick = picker(width, head, True)
            q_head = plain(q_ref[begin : begin + rows, :], q_pick).astype(bf16)
            g_head = plain(g_ref[begin : begin + rows, :], picker(width, head, False)).astype(bf16)
            keys_here = k_ref[low : low + keys, :]
            scores = by_rows(q_head, keys_here) + bias[:, :keys]
            probs = jnp.exp(scores - log_ref[head, begin : begin + rows, 0:1])
            d_probs = by_rows(g_head, v_ref[low : low + keys, :])
            pushed = probs * d_probs
            delta = jnp.sum(pushed, axis=-1, keepdims=True)
            d_raw = (pushed - probs * delta).astype(bf16)
            d_query = plain(d_raw, keys_here) * (HEAD_DIM ** (-0.5))
            acc[...] += by_rows(d_query.astype(bf16), q_pick)
            dk[low : low + keys, :] += contract_first(d_raw, q_head)
            dv[low : low + keys, :] += contract_first(probs.astype(bf16), g_head)

        dq_ref[begin : begin + rows, :] = acc[...].astype(bf16)
    dk_ref[...] = dk[...].astype(bf16)
    dv_ref[...] = dv[...].astype(bf16)


def attend_back(ends, query, key, value, grad, logs):
    total_len, width = query.shape
    heads = width // HEAD_DIM
    rows, spans = row_blocks(total_len)
    most = max(keys for _, _, keys in spans)
    return call(
        backward_kernel,
        (ends,),
        (query, key, value, grad, logs),
        (
            shaped((total_len, width), bf16),
            shaped((total_len, HEAD_DIM), bf16),
            shaped((total_len, HEAD_DIM), bf16),
        ),
        [
            pltpu.VMEM((rows, most), f32),
            pltpu.VMEM((rows, width), f32),
            pltpu.VMEM((total_len, HEAD_DIM), f32),
            pltpu.VMEM((total_len, HEAD_DIM), f32),
        ],
        10 * heads * total_len * total_len * HEAD_DIM,
        "attend_back",
        docs=ends.shape[0],
    )


def turn_kernel(order_ref, dq_ref, dk_ref, dv_ref, cos_ref, sin_ref, pick_ref, out_ref, *, blocks):
    total_len, width = dq_ref.shape
    local = total_len // blocks

    @pl.loop(0, blocks)
    def _(i):
        source = pl.ds(pl.multiple_of(order_ref[i] * local, local), local)
        target = pl.ds(pl.multiple_of(i * local, local), local)
        cos_tab, sin_tab = cos_ref[target, :], sin_ref[target, :]
        dq, dk = dq_ref[source, :].astype(f32), dk_ref[source, :].astype(f32)
        turned = jnp.concatenate(
            [
                *turn_back(dq[:, : width // 2], dq[:, width // 2 :], cos_tab, sin_tab),
                *turn_back(dk[:, :HALF], dk[:, HALF:], cos_tab[:, :HALF], sin_tab[:, :HALF]),
                dv_ref[source, :].astype(f32),
            ],
            axis=1,
        ).astype(bf16)
        out_ref[target, :] = plain(turned, pick_ref[...]).astype(bf16)


def project_kernel(order_ref, mixed_ref, token_ref, gain_ref, *refs, blocks):
    weight_refs = refs[:blocks]
    hidden_ref, normed_ref, flat_ref = refs[blocks:]
    local = token_ref.shape[0]
    group_width = mixed_ref.shape[2]
    depth = weight_refs[0].shape[0]
    for g in range(blocks):
        flat_ref[:, g * group_width : (g + 1) * group_width] = mixed_ref[g]
    for i in range(blocks):
        here = pl.ds(pl.multiple_of(order_ref[i] * depth, depth), depth)
        hidden_ref[:, here] = by_rows(flat_ref[...], weight_refs[i][...]) + token_ref[
            :, here
        ].astype(f32)
    few = 32

    @pl.loop(0, local // few)
    def _(step):
        here = pl.ds(pl.multiple_of(step * few, few), few)
        values = hidden_ref[here, :]
        scale = lax.rsqrt(jnp.mean(values * values, axis=-1, keepdims=True) + norm_eps)
        normed_ref[here, :] = (values * scale * gain_ref[1:2, :]).astype(bf16)


def branch_kernel(order_ref, grad_ref, hidden_ref, cot_ref, gain_ref, *refs, blocks):
    weight_refs = refs[:blocks]
    d_hidden_ref, d_mixed_ref, d_branch_ref, gain_out_ref, branch, acc = refs[blocks:]
    local, width = grad_ref.shape
    depth = weight_refs[0].shape[0]
    group_width = d_mixed_ref.shape[2]
    few = 32
    gain_out_ref[...] = jnp.zeros_like(gain_out_ref)

    @pl.loop(0, local // few)
    def _(step):
        here = pl.ds(pl.multiple_of(step * few, few), few)
        values, grads = hidden_ref[here, :], grad_ref[here, :]
        scale = lax.rsqrt(jnp.mean(values * values, axis=-1, keepdims=True) + norm_eps)
        unit = values * scale
        gain_out_ref[0:1, :] += jnp.sum(grads * unit, axis=0, keepdims=True)
        pushed = grads * gain_ref[1:2, :]
        part = scale * (pushed - unit * jnp.mean(pushed * unit, axis=-1, keepdims=True))
        d_hidden = cot_ref[here, :].astype(f32) + part
        d_hidden_ref[here, :] = d_hidden
        branch[here, :] = d_hidden.astype(bf16)

    for i in range(blocks):
        here = pl.ds(pl.multiple_of(order_ref[i] * depth, depth), depth)
        piece = branch[:, here]
        d_branch_ref[order_ref[i]] = piece
        part = plain(piece, weight_refs[i][...])
        if i == 0:
            acc[...] = part
        else:
            acc[...] += part
    for g in range(blocks):
        d_mixed_ref[g] = acc[:, g * group_width : (g + 1) * group_width].astype(bf16)


def outer_kernel(order_ref, grad_ref, *refs, blocks):
    mixed_refs, out_ref = refs[:blocks], refs[blocks]
    for i in range(blocks):
        part = contract_first(grad_ref[order_ref[i]], mixed_refs[i][...])
        if i == 0:
            out_ref[...] = part
        else:
            out_ref[...] += part


def shards(
    tokens,
    doc_lengths,
    query_weight,
    key_weight,
    value_weight,
    output_weight,
    gate_weight,
    up_weight,
    down_weight,
    attn_gain,
    mlp_gain,
    cotangent,
):
    groups = lax.axis_size("seq")
    dp_count = lax.axis_size("dp")
    my_index = lax.axis_index("seq")
    my_seq = lax.axis_index("dp")
    local_len, width = tokens.shape[1:]
    total_len = local_len * groups
    per_group = HEADS // groups
    copies = groups // KV_HEADS
    group_width = per_group * HEAD_DIM
    all_heads = HEADS * HEAD_DIM
    gain_rows = attn_gain.shape[0]
    kv_rows = HEAD_DIM // copies
    q_rows, k_rows = query_weight.shape[0], key_weight.shape[0]
    ring_rows = q_rows + 2 * k_rows
    half = groups // 2
    share = (dp_count - 1) * total_len <= 3 * gate_weight.shape[0]
    my_place = my_index * dp_count + my_seq

    order = jnp.asarray([order_of(i, groups) for i in range(groups)], jnp.int32)[my_index]
    here = my_seq.reshape(1).astype(jnp.int32)
    token_bf, cot_bf = tokens[0], cotangent[0]

    rows_here = jnp.concatenate([query_weight, key_weight, value_weight], axis=0)
    ring = far_gather(rows_here, dp_count)
    token_pieces = gather_pieces(token_bf, groups)
    gains = sum_everywhere(
        lax.dynamic_update_slice(
            jnp.zeros((2, width), bf16),
            jnp.stack([attn_gain, mlp_gain]),
            (0, my_place * gain_rows),
        ),
        groups,
        dp_count,
    ).astype(f32)
    pair_rows = None
    copy_index = lax.rem(my_index, copies)
    if copies > 1:
        in_ring = in_order(ring, dp_count).reshape(dp_count, ring_rows, width)
        own = jnp.stack(
            [
                in_ring[:, q_rows : q_rows + k_rows].reshape(kv_rows, width),
                in_ring[:, q_rows + k_rows :].reshape(kv_rows, width),
            ]
        )
        parts = [own]
        for bit in range(copies.bit_length() - 1):
            parts = parts + [
                lax.ppermute(part, "seq", [(i, i ^ (1 << bit)) for i in range(groups)])
                for part in parts
            ]
        stacked = jnp.stack(parts)
        pair_rows = jnp.concatenate(
            [
                lax.dynamic_index_in_dim(
                    stacked, jnp.bitwise_xor(copy_index, i), 0, keepdims=False
                )
                for i in range(copies)
            ],
            axis=1,
        ).reshape(2 * HEAD_DIM, width)

    ends = jnp.cumsum(doc_lengths[0], dtype=jnp.int32)
    places = (order[:, None] * local_len + jnp.arange(local_len, dtype=jnp.int32)[None]).reshape(-1)
    begins = jnp.max(jnp.where(places[:, None] >= ends[None, :], ends[None, :], 0), axis=1)
    cos_tab, sin_tab = rope_tables(places - begins)
    cos_wide, sin_wide = jnp.tile(cos_tab, (1, per_group)), jnp.tile(sin_tab, (1, per_group))

    cot_pieces = gather_pieces(hold(cot_bf, token_pieces[1], token_pieces[2]), groups)
    output_ring = far_gather(hold(output_weight, token_pieces[3]), dp_count)
    normed_all, query, key, value = project_in(
        order, here, token_pieces, ring, pair_rows, gains, cos_wide, sin_wide,
        group_width, q_rows, k_rows,
    )
    output_rows = in_order(output_ring, dp_count)
    output_pieces = gather_pieces(hold(output_rows, cot_pieces[3]), groups)
    mixed_heads, logs = attend(ends, query, key, value)
    mixed = lax.all_to_all(
        mixed_heads.reshape(groups, local_len, group_width),
        "seq",
        split_axis=0,
        concat_axis=0,
        tiled=True,
    )

    hidden_state, normed_two, mixed_flat = call(
        project_kernel,
        (order,),
        (mixed, token_bf, gains, *output_pieces),
        (
            shaped((local_len, width), f32),
            shaped((local_len, width), bf16),
            shaped((local_len, all_heads), bf16),
        ),
        [],
        2 * local_len * width * all_heads,
        "project",
        blocks=groups,
    )
    normed_two_pieces = gather_pieces(normed_two, groups)
    if share:
        cot_far = far_gather(hold(cot_bf, output_ring[-1], output_ring[-2]), dp_count)[1:]
        normed_far = far_gather(normed_two, dp_count)[1:]
        far_cot_pieces = gather_pieces(
            hold(jnp.concatenate(cot_far, axis=0), normed_two_pieces[3]), groups
        )

    def forward_mlp(normed_toks, cot_toks):
        gate_val = by_rows(normed_toks, gate_weight)
        up_val = by_rows(normed_toks, up_weight)
        sigmoid_val = 1.0 / (1.0 + jnp.exp(-gate_val))
        active = (gate_val * sigmoid_val * up_val).astype(bf16)
        d_active = by_rows(cot_toks, down_weight)
        d_gate, d_up = gate_grads(d_active, gate_val, up_val, sigmoid_val)
        return active, d_gate, d_up

    cot_all = jnp.concatenate(cot_pieces, axis=0)
    normed_two_all = jnp.concatenate(normed_two_pieces, axis=0)
    active, d_gate, d_up = forward_mlp(normed_two_all, cot_all)
    d_blocks = (
        (plain(d_gate, gate_weight) + plain(d_up, up_weight))
        .astype(bf16)
        .reshape(groups, local_len, width)
    )
    d_normed_two = scatter_blocks(d_blocks[:half], d_blocks[half:], groups)
    grad_gate = by_tokens(d_gate, normed_two_all)
    grad_up = by_tokens(d_up, normed_two_all)
    grad_down = by_tokens(active, cot_all)
    mlp_blocks = plain(active, down_weight).astype(bf16).reshape(groups, local_len, width)
    d_normed_two, grad_gate, grad_up, grad_down, mlp_blocks = lax.optimization_barrier(
        (d_normed_two, grad_gate, grad_up, grad_down, mlp_blocks)
    )
    if share:
        far_normed_pieces = gather_pieces(
            hold(jnp.concatenate(normed_far, axis=0), far_cot_pieces[3], d_normed_two), groups
        )
    mixed_pieces = gather_pieces(
        hold(mixed_flat, *([far_normed_pieces[3]] if share else [d_normed_two])), groups
    )

    d_hidden, d_mixed, d_branch, grad_mlp_gain = call(
        branch_kernel,
        (order,),
        (d_normed_two, hidden_state, cot_bf, gains, *output_pieces),
        (
            shaped((local_len, width), f32),
            shaped((groups, local_len, group_width), bf16),
            shaped((groups, local_len, output_rows.shape[0]), bf16),
            shaped((1, width), f32),
        ),
        [pltpu.VMEM((local_len, width), bf16), pltpu.VMEM((local_len, all_heads), f32)],
        2 * local_len * width * all_heads,
        "branch",
        blocks=groups,
    )
    d_mixed_heads = lax.all_to_all(
        d_mixed, "seq", split_axis=0, concat_axis=0, tiled=True
    ).reshape(total_len, group_width)
    d_branch_cols = lax.all_to_all(d_branch, "seq", split_axis=0, concat_axis=0, tiled=True)

    grad_output = call(
        outer_kernel,
        (order,),
        (d_branch_cols, *mixed_pieces),
        (shaped((output_rows.shape[0], all_heads), f32),),
        [],
        2 * total_len * output_rows.shape[0] * all_heads,
        "outer",
        blocks=groups,
    )[0].reshape(dp_count, -1, all_heads)
    out_parts = far_send(
        [
            lax.dynamic_index_in_dim(
                grad_output, jnp.bitwise_xor(my_seq, k), 0, keepdims=False
            )
            for k in range(dp_count)
        ],
        dp_count,
    )

    d_query, d_key, d_value = attend_back(ends, query, key, value, d_mixed_heads, logs)
    if copies > 1:
        total_pair = jnp.stack([d_key, d_value]).astype(f32)
        for bit in range(copies.bit_length() - 1):
            total_pair = total_pair + lax.ppermute(
                total_pair, "seq", [(i, i ^ (1 << bit)) for i in range(groups)]
            )
        d_key, d_value = total_pair[0], total_pair[1]

    column = jnp.arange(dp_count * ring_rows, dtype=jnp.int32)
    block = jnp.bitwise_xor(my_seq, column // ring_rows)
    within = column % ring_rows
    row = block * q_rows + within
    from_query = (
        (row % HEAD_DIM) // HALF * (group_width // 2) + row // HEAD_DIM * HALF + row % HALF
    )
    pair = (within - q_rows) // k_rows
    from_pair = (
        group_width
        + pair * HEAD_DIM
        + copy_index * kv_rows
        + block * k_rows
        + (within - q_rows) % k_rows
    )
    source = jnp.where(within < q_rows, from_query, from_pair)
    pick = (
        jnp.arange(group_width + 2 * HEAD_DIM, dtype=jnp.int32)[:, None] == source[None, :]
    ).astype(bf16)
    d_lin = call(
        turn_kernel,
        (order,),
        (d_query, d_key, d_value, cos_wide, sin_wide, pick),
        (shaped((total_len, dp_count * ring_rows), bf16),),
        [],
        2 * total_len * dp_count * ring_rows * (group_width + 2 * HEAD_DIM),
        "turn",
        blocks=groups,
    )[0]
    d_normed_part = plain(d_lin, jnp.concatenate(ring, axis=0)).astype(bf16)
    grad_attn_gain = jnp.sum(d_normed_part.astype(f32) * normed_all.astype(f32), axis=0) / gains[0]
    d_normed_part = d_normed_part.reshape(groups, local_len, width)
    row_parts = far_send(
        list(by_tokens(d_lin, normed_all).reshape(dp_count, ring_rows, width)), dp_count
    )
    gain_grads = jnp.stack([grad_attn_gain, grad_mlp_gain[0]])

    scatter_one = scatter_steps(d_normed_part[:half], d_normed_part[half:], groups)
    scatter_two = scatter_steps(mlp_blocks[:half], mlp_blocks[half:], groups)
    gain_steps = sum_steps(gain_grads, groups, dp_count)
    if share:
        far_cot = jnp.concatenate(far_cot_pieces, axis=0)
        far_normed = jnp.concatenate(far_normed_pieces, axis=0)
        now = next(scatter_one)
        gate_val = by_rows(hold(far_normed, now), gate_weight)
        now = scatter_one.send(gate_val)
        up_val = by_rows(hold(far_normed, now, gain_steps.send(None)), up_weight)
        now = scatter_one.send(up_val)
        d_active = by_rows(hold(far_cot, now, gain_steps.send(up_val)), down_weight)
        sigmoid_val = 1.0 / (1.0 + jnp.exp(-gate_val))
        far_active = (gate_val * sigmoid_val * up_val).astype(bf16)
        far_gate, far_up = gate_grads(d_active, gate_val, up_val, sigmoid_val)
        d_normed = scatter_one.send(far_up)
        now = next(scatter_two)
        grad_gate = grad_gate + by_tokens(
            hold(far_gate, d_normed, now, gain_steps.send(far_up)), far_normed
        )
        now = scatter_two.send(grad_gate)
        grad_up = grad_up + by_tokens(hold(far_up, now, gain_steps.send(grad_gate)), far_normed)
        now = scatter_two.send(grad_up)
        grad_down = grad_down + by_tokens(
            hold(far_active, now, gain_steps.send(grad_up)), far_cot
        )
        mlp_out = scatter_two.send(grad_down)
        gain_grads = gain_steps.send(grad_down)
    else:
        grad_gate, grad_up, grad_down = (
            lax.psum(grad.astype(bf16), "dp").astype(f32) for grad in (grad_gate, grad_up, grad_down)
        )
        d_normed, mlp_out, gain_grads = (run_steps(g) for g in (scatter_one, scatter_two, gain_steps))
    result = (hidden_state + mlp_out).astype(bf16)
    inputs = token_bf.astype(f32)
    _, norm_one_back = jax.vjp(lambda v: rms_norm(v, gains[0]), inputs)
    d_input = (d_hidden + norm_one_back(d_normed)[0]).astype(bf16)
    grad_output, grad_rows = far_sum(out_parts), far_sum(row_parts)
    gain_grads = lax.dynamic_slice(gain_grads, (0, my_place * gain_rows), (2, gain_rows))

    return (
        result[None],
        d_input[None],
        grad_rows[:q_rows],
        grad_rows[q_rows : q_rows + k_rows],
        grad_rows[q_rows + k_rows :],
        grad_output,
        grad_gate,
        grad_up,
        grad_down,
        gain_grads[0],
        gain_grads[1],
    )


def solution(mesh):
    in_specs = (
        P("dp", "seq", None),
        P("dp", None),
        P(("seq", "dp"), None),
        P(("seq", "dp"), None),
        P(("seq", "dp"), None),
        P(("seq", "dp"), None),
        P("seq", None),
        P("seq", None),
        P("seq", None),
        P(("seq", "dp")),
        P(("seq", "dp")),
        P("dp", "seq", None),
    )
    out_specs = (
        P("dp", "seq", None),
        P("dp", "seq", None),
        P(("seq", "dp"), None),
        P(("seq", "dp"), None),
        P(("seq", "dp"), None),
        P(("seq", "dp"), None),
        P("seq", None),
        P("seq", None),
        P("seq", None),
        P(("seq", "dp")),
        P(("seq", "dp")),
    )
    return jax.shard_map(shards, mesh=mesh, in_specs=in_specs, out_specs=out_specs, check_vma=False)
```

```python
import functools
import math

import jax
import jax.numpy as jnp
from jax import lax
from jax.experimental import pallas as pl
from jax.experimental.pallas import tpu as pltpu
from jax.sharding import PartitionSpec as P

HEADS = 32
KV_HEADS = 8
HEAD_DIM = 64
HALF = HEAD_DIM // 2
NEG = -1e30

norm_eps = 1e-05
bf16 = jnp.bfloat16
f32 = jnp.float32


def by_rows(left, weight_mat):
    return lax.dot_general(
        left, weight_mat, (((1,), (1,)), ((), ())), preferred_element_type=f32
    )


def by_tokens(left, right):
    return lax.dot_general(
        left, right, (((0,), (0,)), ((), ())), preferred_element_type=f32
    )


def plain(left, right):
    return jnp.dot(left, right, preferred_element_type=f32)


def rms_norm(values, gain_vec):
    return (
        values * lax.rsqrt(jnp.mean(values * values, axis=-1, keepdims=True) + norm_eps) * gain_vec
    )


def rope_tables(positions):
    exponent = jnp.arange(HALF, dtype=f32) * 2.0 / HEAD_DIM
    inverse = 1.0 / 500000.0**exponent
    wavelen = 2.0 * math.pi / inverse
    scaled = jnp.where(wavelen > 8192.0, inverse / 32.0, inverse)
    smooth = (8192.0 / wavelen - 1.0) / 3.0
    smoothed = (1.0 - smooth) * scaled / 32.0 + smooth * scaled
    medium = (wavelen >= 2048.0) & (wavelen <= 8192.0)
    inverse = jnp.where(medium, smoothed, scaled)
    angles = positions.astype(f32)[:, None] * inverse[None, :]
    return (jnp.cos(angles), jnp.sin(angles))


def turn(first, second, cos_tab, sin_tab):
    return (first * cos_tab - second * sin_tab, second * cos_tab + first * sin_tab)


def turn_back(first, second, cos_tab, sin_tab):
    return (first * cos_tab + second * sin_tab, second * cos_tab - first * sin_tab)


def hold(values, *others):
    return lax.optimization_barrier((values, *others))[0] if others else values


def gate_grads(d_active, gate_val, up_val, sigmoid_val):
    d_gate = (d_active * up_val * sigmoid_val * (1.0 + gate_val * (1.0 - sigmoid_val))).astype(bf16)
    d_up = (d_active * gate_val * sigmoid_val).astype(bf16)
    return (d_gate, d_up)


def hops(index, count):
    if count == 8:
        return (2, 4) if index % 2 == 0 else (4, 2)
    return tuple(1 << bit for bit in range(1, count.bit_length() - 1))


def half_order(index, count):
    blocks = [index]
    for hop in hops(index, count):
        blocks = blocks + [block ^ hop for block in blocks]
    return blocks


def order_of(index, count):
    return half_order(index, count) + half_order(index ^ 1, count)


def swap(values, count, stage):
    if stage < 0:
        perm = [(i, i ^ 1) for i in range(count)]
    else:
        perm = [(i, i ^ hops(i, count)[stage]) for i in range(count)]
    return lax.ppermute(values, "seq", perm)


def gather_pieces(values, count, *after):
    def later(pieces):
        return [pieces[0]] + [hold(piece, *after) if after else piece for piece in pieces[1:]]

    pieces = [values]
    for stage in range(len(hops(0, count))):
        pieces = pieces + [swap(piece, count, stage) for piece in later(pieces)]
    return pieces + [swap(piece, count, -1) for piece in later(pieces)]


def scatter_steps(mine, theirs, count):
    half = mine.shape[0]
    arrived = swap(theirs, count, -1)
    total = mine.astype(f32)
    for stage in reversed(range(len(hops(0, count)))):
        after = yield theirs
        total = total + (arrived if after is None else hold(arrived, after)).astype(f32)
        half = half // 2
        theirs = total[half:].astype(bf16)
        total = total[:half]
        arrived = swap(theirs, count, stage)
    after = yield theirs
    total = total + (arrived if after is None else hold(arrived, after)).astype(f32)
    yield total[0]


def run_steps(steps, after=None):
    last = steps.send(after)
    for last in steps:
        pass
    return last


def across(values, count, k):
    return lax.ppermute(values, "dp", [(i, i ^ k) for i in range(count)])


def far_gather(values, count):
    return [values] + [across(values, count, k) for k in range(1, count)]


def in_order(pieces, count):
    here = lax.axis_index("dp")
    rows = pieces[0].shape[0]
    whole = jnp.zeros((count * rows, *pieces[0].shape[1:]), pieces[0].dtype)
    for k, piece in enumerate(pieces):
        whole = lax.dynamic_update_slice_in_dim(whole, piece, jnp.bitwise_xor(here, k) * rows, 0)
    return whole


def far_send(blocks, count):
    return [blocks[0]] + [across(blocks[k].astype(bf16), count, k) for k in range(1, count)]


def far_sum(parts):
    total = parts[0]
    for part in parts[1:]:
        total = total + part.astype(f32)
    return total


def smem():
    return pl.BlockSpec(memory_space=pltpu.SMEM)


def vmem():
    return pl.BlockSpec(memory_space=pltpu.VMEM)


def shaped(shape, dtype):
    return jax.ShapeDtypeStruct(shape, dtype)


def call(body, scalars, arrays, outs, scratch, flops, name, **static):
    moved = sum(math.prod(x.shape) * x.dtype.itemsize for x in (*arrays, *outs))
    return pl.pallas_call(
        functools.partial(body, **static),
        out_shape=tuple(outs),
        in_specs=[smem()] * len(scalars) + [vmem()] * len(arrays),
        out_specs=tuple(vmem() for _ in outs),
        scratch_shapes=scratch,
        cost_estimate=pl.CostEstimate(flops=flops, bytes_accessed=moved, transcendentals=0),
        name=name,
    )(*scalars, *arrays)


def picker(width, head, halves):
    lane = lax.broadcasted_iota(jnp.int32, (width, HEAD_DIM), 0)
    part = lax.broadcasted_iota(jnp.int32, (width, HEAD_DIM), 1)
    if halves:
        target = (part // HALF) * (width // 2) + head * HALF + part % HALF
    else:
        target = head * HEAD_DIM + part
    return jnp.where(lane == target, 1.0, 0.0).astype(bf16)


def tile_bias(ends_ref, docs, row_begin, rows, key_begin, keys):
    row = row_begin + lax.broadcasted_iota(jnp.int32, (rows, 1), 0)
    doc_begin = jnp.zeros((rows, 1), jnp.int32)
    for j in range(docs):
        doc_begin = jnp.maximum(doc_begin, jnp.where(row >= ends_ref[j], ends_ref[j], 0))
    key = key_begin + lax.broadcasted_iota(jnp.int32, (rows, keys), 1)
    return jnp.where((key >= doc_begin) & (key <= row), 0.0, NEG)


def row_blocks(total_len):
    rows = min(256, total_len)
    window = total_len // 2
    spans = []
    for begin in range(0, total_len, rows):
        low = max(0, (begin - window + 1) // rows * rows)
        spans.append((begin, low, begin + rows - low))
    return rows, spans


def contract_first(left, right):
    return lax.dot_general(left, right, (((0,), (0,)), ((), ())), preferred_element_type=f32)


def input_kernel(*refs, blocks, ring, q_rows, k_rows, paired):
    order_ref, dp_ref = refs[:2]
    token_refs = refs[2 : 2 + blocks]
    ring_refs = refs[2 + blocks : 2 + blocks + ring]
    rest = refs[2 + blocks + ring :]
    pair_ref, rest = (rest[0], rest[1:]) if paired else (None, rest)
    gain_ref, cos_ref, sin_ref = rest[:3]
    normed_ref, q_ref, k_ref, v_ref, lin_rows = rest[3:]
    total_len, width = q_ref.shape
    local = total_len // blocks
    chunk = min(q_rows, HALF)
    for k in range(ring):
        block = jnp.bitwise_xor(dp_ref[0], k)
        for j in range(q_rows // chunk):
            row = block * q_rows + j * chunk
            target = (
                lax.div(lax.rem(row, HEAD_DIM), HALF) * (width // 2)
                + lax.div(row, HEAD_DIM) * HALF
                + lax.rem(row, HALF)
            )
            lin_rows[pl.ds(pl.multiple_of(target, chunk), chunk), :] = ring_refs[k][
                j * chunk : (j + 1) * chunk, :
            ]
        if not paired:
            for part in range(2):
                target = width + part * HEAD_DIM + block * k_rows
                source = q_rows + part * k_rows
                lin_rows[pl.ds(pl.multiple_of(target, k_rows), k_rows), :] = ring_refs[k][
                    source : source + k_rows, :
                ]
    if paired:
        lin_rows[width:, :] = pair_ref[...]

    few = 32
    for i in range(blocks):

        @pl.loop(0, local // few)
        def _(step, i=i):
            begin = pl.multiple_of(step * few, few)
            values = token_refs[i][pl.ds(begin, few), :].astype(f32)
            scale = lax.rsqrt(jnp.mean(values * values, axis=-1, keepdims=True) + norm_eps)
            normed_ref[pl.ds(pl.multiple_of(i * local + begin, few), few), :] = (
                values * scale * gain_ref[0:1, :]
            ).astype(bf16)

    many = min(256, total_len)

    @pl.loop(0, total_len // many)
    def _(step):
        here = pl.ds(pl.multiple_of(step * many, many), many)
        lin = by_rows(normed_ref[here, :], lin_rows[...])
        cos_tab, sin_tab = cos_ref[here, :], sin_ref[here, :]
        query = jnp.concatenate(
            turn(lin[:, : width // 2], lin[:, width // 2 : width], cos_tab, sin_tab), axis=1
        )
        query = (query * HEAD_DIM ** (-0.5)).astype(bf16)
        key = jnp.concatenate(
            turn(
                lin[:, width : width + HALF],
                lin[:, width + HALF : width + HEAD_DIM],
                cos_tab[:, :HALF],
                sin_tab[:, :HALF],
            ),
            axis=1,
        ).astype(bf16)
        value = lin[:, width + HEAD_DIM :].astype(bf16)
        for j in range(many // local):
            target = pl.ds(
                pl.multiple_of(order_ref[step * (many // local) + j] * local, local), local
            )
            q_ref[target, :] = query[j * local : (j + 1) * local]
            k_ref[target, :] = key[j * local : (j + 1) * local]
            v_ref[target, :] = value[j * local : (j + 1) * local]


def attend_kernel(ends_ref, q_ref, k_ref, v_ref, o_ref, log_ref, bias, acc, *, docs):
    total_len, width = q_ref.shape
    rows, spans = row_blocks(total_len)
    for begin, low, keys in spans:
        bias[:, :keys] = tile_bias(ends_ref, docs, begin, rows, low, keys)
        acc[...] = jnp.zeros_like(acc)

        @pl.loop(0, width // HEAD_DIM)
        def _(head, begin=begin, low=low, keys=keys):
            q_head = plain(q_ref[begin : begin + rows, :], picker(width, head, True)).astype(bf16)
            scores = by_rows(q_head, k_ref[low : low + keys, :]) + bias[:, :keys]
            peak = jnp.max(scores, axis=-1, keepdims=True)
            probs = jnp.exp(scores - peak)
            total = jnp.sum(probs, axis=-1, keepdims=True)
            mixed = plain(probs.astype(bf16), v_ref[low : low + keys, :]) / total
            acc[...] += by_rows(mixed.astype(bf16), picker(width, head, False))
            log_ref[head, begin : begin + rows, :] = jnp.broadcast_to(
                peak + jnp.log(total), (rows, 128)
            )

        o_ref[begin : begin + rows, :] = acc[...].astype(bf16)


def project_in(order, here, pieces, ring, pair_rows, gains, cos_wide, sin_wide, group_width, q_rows, k_rows):
    blocks = len(pieces)
    local, width = pieces[0].shape
    total_len = blocks * local
    pair = [] if pair_rows is None else [pair_rows]
    return call(
        input_kernel,
        (order, here),
        (*pieces, *ring, *pair, gains, cos_wide, sin_wide),
        (
            shaped((total_len, width), bf16),
            shaped((total_len, group_width), bf16),
            shaped((total_len, HEAD_DIM), bf16),
            shaped((total_len, HEAD_DIM), bf16),
        ),
        [pltpu.VMEM((group_width + 2 * HEAD_DIM, width), bf16)],
        2 * total_len * width * (group_width + 128),
        "project_in",
        blocks=blocks,
        ring=len(ring),
        q_rows=q_rows,
        k_rows=k_rows,
        paired=bool(pair),
    )


def attend(ends, query, key, value):
    total_len, group_width = query.shape
    heads = group_width // HEAD_DIM
    rows, spans = row_blocks(total_len)
    most = max(keys for _, _, keys in spans)
    return call(
        attend_kernel,
        (ends,),
        (query, key, value),
        (shaped((total_len, group_width), bf16), shaped((heads, total_len, 128), f32)),
        [pltpu.VMEM((rows, most), f32), pltpu.VMEM((rows, group_width), f32)],
        8 * heads * total_len * total_len * HEAD_DIM,
        "attend",
        docs=ends.shape[0],
    )


def backward_kernel(
    ends_ref, q_ref, k_ref, v_ref, g_ref, log_ref, dq_ref, dk_ref, dv_ref, bias, acc, dk, dv, *, docs
):
    total_len, width = q_ref.shape
    rows, spans = row_blocks(total_len)
    dk[...] = jnp.zeros_like(dk)
    dv[...] = jnp.zeros_like(dv)
    for begin, low, keys in spans:
        bias[:, :keys] = tile_bias(ends_ref, docs, begin, rows, low, keys)
        acc[...] = jnp.zeros_like(acc)

        @pl.loop(0, width // HEAD_DIM)
        def _(head, begin=begin, low=low, keys=keys):
            q_pick = picker(width, head, True)
            q_head = plain(q_ref[begin : begin + rows, :], q_pick).astype(bf16)
            g_head = plain(g_ref[begin : begin + rows, :], picker(width, head, False)).astype(bf16)
            keys_here = k_ref[low : low + keys, :]
            scores = by_rows(q_head, keys_here) + bias[:, :keys]
            probs = jnp.exp(scores - log_ref[head, begin : begin + rows, 0:1])
            d_probs = by_rows(g_head, v_ref[low : low + keys, :])
            pushed = probs * d_probs
            delta = jnp.sum(pushed, axis=-1, keepdims=True)
            d_raw = (pushed - probs * delta).astype(bf16)
            d_query = plain(d_raw, keys_here) * (HEAD_DIM ** (-0.5))
            acc[...] += by_rows(d_query.astype(bf16), q_pick)
            dk[low : low + keys, :] += contract_first(d_raw, q_head)
            dv[low : low + keys, :] += contract_first(probs.astype(bf16), g_head)

        dq_ref[begin : begin + rows, :] = acc[...].astype(bf16)
    dk_ref[...] = dk[...].astype(bf16)
    dv_ref[...] = dv[...].astype(bf16)


def attend_back(ends, query, key, value, grad, logs):
    total_len, width = query.shape
    heads = width // HEAD_DIM
    rows, spans = row_blocks(total_len)
    most = max(keys for _, _, keys in spans)
    return call(
        backward_kernel,
        (ends,),
        (query, key, value, grad, logs),
        (
            shaped((total_len, width), bf16),
            shaped((total_len, HEAD_DIM), bf16),
            shaped((total_len, HEAD_DIM), bf16),
        ),
        [
            pltpu.VMEM((rows, most), f32),
            pltpu.VMEM((rows, width), f32),
            pltpu.VMEM((total_len, HEAD_DIM), f32),
            pltpu.VMEM((total_len, HEAD_DIM), f32),
        ],
        10 * heads * total_len * total_len * HEAD_DIM,
        "attend_back",
        docs=ends.shape[0],
    )


def turn_kernel(order_ref, dq_ref, dk_ref, dv_ref, cos_ref, sin_ref, pick_ref, out_ref, *, blocks):
    total_len, width = dq_ref.shape
    local = total_len // blocks

    @pl.loop(0, blocks)
    def _(i):
        source = pl.ds(pl.multiple_of(order_ref[i] * local, local), local)
        target = pl.ds(pl.multiple_of(i * local, local), local)
        cos_tab, sin_tab = cos_ref[target, :], sin_ref[target, :]
        dq, dk = dq_ref[source, :].astype(f32), dk_ref[source, :].astype(f32)
        turned = jnp.concatenate(
            [
                *turn_back(dq[:, : width // 2], dq[:, width // 2 :], cos_tab, sin_tab),
                *turn_back(dk[:, :HALF], dk[:, HALF:], cos_tab[:, :HALF], sin_tab[:, :HALF]),
                dv_ref[source, :].astype(f32),
            ],
            axis=1,
        ).astype(bf16)
        out_ref[target, :] = plain(turned, pick_ref[...]).astype(bf16)


def project_kernel(order_ref, mixed_ref, token_ref, gain_ref, *refs, blocks):
    weight_refs = refs[:blocks]
    hidden_ref, normed_ref, flat_ref = refs[blocks:]
    local = token_ref.shape[0]
    group_width = mixed_ref.shape[2]
    depth = weight_refs[0].shape[0]
    for g in range(blocks):
        flat_ref[:, g * group_width : (g + 1) * group_width] = mixed_ref[g]
    for i in range(blocks):
        here = pl.ds(pl.multiple_of(order_ref[i] * depth, depth), depth)
        hidden_ref[:, here] = by_rows(flat_ref[...], weight_refs[i][...]) + token_ref[
            :, here
        ].astype(f32)
    few = 32

    @pl.loop(0, local // few)
    def _(step):
        here = pl.ds(pl.multiple_of(step * few, few), few)
        values = hidden_ref[here, :]
        scale = lax.rsqrt(jnp.mean(values * values, axis=-1, keepdims=True) + norm_eps)
        normed_ref[here, :] = (values * scale * gain_ref[1:2, :]).astype(bf16)


def branch_kernel(order_ref, grad_ref, hidden_ref, cot_ref, gain_ref, *refs, blocks):
    weight_refs = refs[:blocks]
    d_hidden_ref, d_mixed_ref, d_branch_ref, gain_out_ref, branch, acc = refs[blocks:]
    local, width = grad_ref.shape
    depth = weight_refs[0].shape[0]
    group_width = d_mixed_ref.shape[2]
    few = 32
    gain_out_ref[...] = jnp.zeros_like(gain_out_ref)

    @pl.loop(0, local // few)
    def _(step):
        here = pl.ds(pl.multiple_of(step * few, few), few)
        values, grads = hidden_ref[here, :], grad_ref[here, :]
        scale = lax.rsqrt(jnp.mean(values * values, axis=-1, keepdims=True) + norm_eps)
        unit = values * scale
        gain_out_ref[0:1, :] += jnp.sum(grads * unit, axis=0, keepdims=True)
        pushed = grads * gain_ref[1:2, :]
        part = scale * (pushed - unit * jnp.mean(pushed * unit, axis=-1, keepdims=True))
        d_hidden = cot_ref[here, :].astype(f32) + part
        d_hidden_ref[here, :] = d_hidden
        branch[here, :] = d_hidden.astype(bf16)

    for i in range(blocks):
        here = pl.ds(pl.multiple_of(order_ref[i] * depth, depth), depth)
        piece = branch[:, here]
        d_branch_ref[order_ref[i]] = piece
        part = plain(piece, weight_refs[i][...])
        if i == 0:
            acc[...] = part
        else:
            acc[...] += part
    for g in range(blocks):
        d_mixed_ref[g] = acc[:, g * group_width : (g + 1) * group_width].astype(bf16)


def outer_kernel(order_ref, grad_ref, *refs, blocks):
    mixed_refs, out_ref = refs[:blocks], refs[blocks]
    for i in range(blocks):
        part = contract_first(grad_ref[order_ref[i]], mixed_refs[i][...])
        if i == 0:
            out_ref[...] = part
        else:
            out_ref[...] += part


def shards(
    tokens,
    doc_lengths,
    query_weight,
    key_weight,
    value_weight,
    output_weight,
    gate_weight,
    up_weight,
    down_weight,
    attn_gain,
    mlp_gain,
    cotangent,
):
    groups = lax.axis_size("seq")
    dp_count = lax.axis_size("dp")
    my_index = lax.axis_index("seq")
    my_seq = lax.axis_index("dp")
    local_len, width = tokens.shape[1:]
    total_len = local_len * groups
    per_group = HEADS // groups
    copies = groups // KV_HEADS
    group_width = per_group * HEAD_DIM
    all_heads = HEADS * HEAD_DIM
    gain_rows = attn_gain.shape[0]
    kv_rows = HEAD_DIM // copies
    q_rows, k_rows = query_weight.shape[0], key_weight.shape[0]
    ring_rows = q_rows + 2 * k_rows
    half = groups // 2
    share = (dp_count - 1) * total_len <= 3 * gate_weight.shape[0]

    order = jnp.asarray([order_of(i, groups) for i in range(groups)], jnp.int32)[my_index]
    here = my_seq.reshape(1).astype(jnp.int32)
    token_bf, cot_bf = tokens[0], cotangent[0]

    rows_here = jnp.concatenate([query_weight, key_weight, value_weight], axis=0)
    ring = far_gather(rows_here, dp_count)
    token_pieces = gather_pieces(token_bf, groups)
    gains = jnp.broadcast_to(
        jnp.concatenate([attn_gain, mlp_gain])[None], (groups * dp_count, 2 * gain_rows)
    )
    gains = lax.all_to_all(gains, ("seq", "dp"), split_axis=0, concat_axis=0, tiled=True)
    gains = jnp.stack(
        [gains[:, :gain_rows].reshape(width), gains[:, gain_rows:].reshape(width)]
    ).astype(f32)
    pair_rows = None
    copy_index = lax.rem(my_index, copies)
    if copies > 1:
        in_ring = in_order(ring, dp_count).reshape(dp_count, ring_rows, width)
        own = jnp.stack(
            [
                in_ring[:, q_rows : q_rows + k_rows].reshape(kv_rows, width),
                in_ring[:, q_rows + k_rows :].reshape(kv_rows, width),
            ]
        )
        parts = [own]
        for bit in range(copies.bit_length() - 1):
            parts = parts + [
                lax.ppermute(part, "seq", [(i, i ^ (1 << bit)) for i in range(groups)])
                for part in parts
            ]
        stacked = jnp.stack(parts)
        pair_rows = jnp.concatenate(
            [
                lax.dynamic_index_in_dim(
                    stacked, jnp.bitwise_xor(copy_index, i), 0, keepdims=False
                )
                for i in range(copies)
            ],
            axis=1,
        ).reshape(2 * HEAD_DIM, width)

    ends = jnp.cumsum(doc_lengths[0], dtype=jnp.int32)
    places = (order[:, None] * local_len + jnp.arange(local_len, dtype=jnp.int32)[None]).reshape(-1)
    begins = jnp.max(jnp.where(places[:, None] >= ends[None, :], ends[None, :], 0), axis=1)
    cos_tab, sin_tab = rope_tables(places - begins)
    cos_wide, sin_wide = jnp.tile(cos_tab, (1, per_group)), jnp.tile(sin_tab, (1, per_group))

    output_ring = far_gather(hold(output_weight, token_pieces[3]), dp_count)
    normed_all, query, key, value = project_in(
        order, here, token_pieces, ring, pair_rows, gains, cos_wide, sin_wide,
        group_width, q_rows, k_rows,
    )
    output_rows = in_order([hold(piece, normed_all) for piece in output_ring], dp_count)
    mixed_heads, logs = attend(ends, hold(query, output_rows), key, value)
    output_pieces = gather_pieces(output_rows, groups, mixed_heads)
    cot_pieces = gather_pieces(
        hold(cot_bf, token_pieces[1], token_pieces[2]), groups, normed_all
    )
    mixed = lax.all_to_all(
        mixed_heads.reshape(groups, local_len, group_width),
        "seq",
        split_axis=0,
        concat_axis=0,
        tiled=True,
    )

    hidden_state, normed_two, mixed_flat = call(
        project_kernel,
        (order,),
        (mixed, token_bf, gains, *output_pieces),
        (
            shaped((local_len, width), f32),
            shaped((local_len, width), bf16),
            shaped((local_len, all_heads), bf16),
        ),
        [],
        2 * local_len * width * all_heads,
        "project",
        blocks=groups,
    )
    normed_two_pieces = gather_pieces(normed_two, groups)
    if share:
        cot_far = far_gather(hold(cot_bf, output_rows), dp_count)[1:]
        normed_far = far_gather(hold(normed_two, normed_two_pieces[1]), dp_count)[1:]

    def forward_mlp(normed_toks, cot_toks):
        gate_val = by_rows(normed_toks, gate_weight)
        up_val = by_rows(normed_toks, up_weight)
        sigmoid_val = 1.0 / (1.0 + jnp.exp(-gate_val))
        active = (gate_val * sigmoid_val * up_val).astype(bf16)
        d_active = by_rows(cot_toks, down_weight)
        d_gate, d_up = gate_grads(d_active, gate_val, up_val, sigmoid_val)
        return active, d_gate, d_up

    cot_all = jnp.concatenate(cot_pieces, axis=0)
    normed_two_all = jnp.concatenate(normed_two_pieces, axis=0)
    active, d_gate, d_up = forward_mlp(normed_two_all, cot_all)
    d_blocks = (
        (plain(d_gate, gate_weight) + plain(d_up, up_weight))
        .astype(bf16)
        .reshape(groups, local_len, width)
    )
    if share:
        far_cot_pieces = gather_pieces(
            hold(jnp.concatenate(cot_far, axis=0), normed_two_pieces[3]), groups, d_blocks
        )
    steps = scatter_steps(d_blocks[:half], d_blocks[half:], groups)
    next(steps)
    now = steps.send(None)
    grad_gate = by_tokens(hold(d_gate, now), normed_two_all)
    grad_up = by_tokens(hold(d_up, grad_gate), normed_two_all)
    now = steps.send(grad_up)
    grad_down = by_tokens(hold(active, now), cot_all)
    d_normed_two = run_steps(steps, grad_down)
    if share:
        far_normed = jnp.concatenate([hold(piece, grad_up) for piece in normed_far], axis=0)

    d_hidden, d_mixed, d_branch, grad_mlp_gain = call(
        branch_kernel,
        (order,),
        (d_normed_two, hidden_state, cot_bf, gains, *output_pieces),
        (
            shaped((local_len, width), f32),
            shaped((groups, local_len, group_width), bf16),
            shaped((groups, local_len, output_rows.shape[0]), bf16),
            shaped((1, width), f32),
        ),
        [pltpu.VMEM((local_len, width), bf16), pltpu.VMEM((local_len, all_heads), f32)],
        2 * local_len * width * all_heads,
        "branch",
        blocks=groups,
    )
    d_mixed_heads = lax.all_to_all(
        d_mixed, "seq", split_axis=0, concat_axis=0, tiled=True
    ).reshape(total_len, group_width)
    mlp_blocks = plain(hold(active, d_mixed), down_weight).astype(bf16)
    mlp_blocks = mlp_blocks.reshape(groups, local_len, width)
    if share:
        far_normed_pieces = gather_pieces(hold(far_normed, d_normed_two), groups, d_mixed)
    d_mixed_heads = hold(d_mixed_heads, mlp_blocks)
    d_branch_cols = lax.all_to_all(d_branch, "seq", split_axis=0, concat_axis=0, tiled=True)

    def output_gradient(*after):
        pieces = gather_pieces(hold(mixed_flat, *after), groups)

        def finish(*after):
            grad = call(
                outer_kernel,
                (order,),
                (hold(d_branch_cols, *after), *pieces),
                (shaped((output_rows.shape[0], all_heads), f32),),
                [],
                2 * total_len * output_rows.shape[0] * all_heads,
                "outer",
                blocks=groups,
            )[0].reshape(dp_count, -1, all_heads)
            return far_send(
                [
                    lax.dynamic_index_in_dim(
                        grad, jnp.bitwise_xor(my_seq, k), 0, keepdims=False
                    )
                    for k in range(dp_count)
                ],
                dp_count,
            )

        return finish

    d_query, d_key, d_value = attend_back(ends, query, key, value, d_mixed_heads, logs)
    if copies > 1:
        total_pair = jnp.stack([d_key, d_value]).astype(f32)
        for bit in range(copies.bit_length() - 1):
            total_pair = total_pair + lax.ppermute(
                total_pair, "seq", [(i, i ^ (1 << bit)) for i in range(groups)]
            )
        d_key, d_value = total_pair[0], total_pair[1]

    column = jnp.arange(dp_count * ring_rows, dtype=jnp.int32)
    block = jnp.bitwise_xor(my_seq, column // ring_rows)
    within = column % ring_rows
    row = block * q_rows + within
    from_query = (
        (row % HEAD_DIM) // HALF * (group_width // 2) + row // HEAD_DIM * HALF + row % HALF
    )
    pair = (within - q_rows) // k_rows
    from_pair = (
        group_width
        + pair * HEAD_DIM
        + copy_index * kv_rows
        + block * k_rows
        + (within - q_rows) % k_rows
    )
    source = jnp.where(within < q_rows, from_query, from_pair)
    pick = (
        jnp.arange(group_width + 2 * HEAD_DIM, dtype=jnp.int32)[:, None] == source[None, :]
    ).astype(bf16)
    d_lin = call(
        turn_kernel,
        (order,),
        (d_query, d_key, d_value, cos_wide, sin_wide, pick),
        (shaped((total_len, dp_count * ring_rows), bf16),),
        [],
        2 * total_len * dp_count * ring_rows * (group_width + 2 * HEAD_DIM),
        "turn",
        blocks=groups,
    )[0]
    d_normed_part = plain(d_lin, jnp.concatenate(ring, axis=0)).astype(bf16)
    grad_attn_gain = jnp.sum(d_normed_part.astype(f32) * normed_all.astype(f32), axis=0) / gains[0]
    d_normed_part = d_normed_part.reshape(groups, local_len, width)
    scatter_one = scatter_steps(d_normed_part[:half], d_normed_part[half:], groups)
    scatter_two = scatter_steps(mlp_blocks[:half], mlp_blocks[half:], groups)
    now = next(scatter_one)
    grad_lin = by_tokens(hold(d_lin, now), normed_all)
    now = scatter_one.send(grad_lin)
    gain_grads = jnp.concatenate(
        [
            grad_attn_gain.reshape(-1, gain_rows),
            grad_mlp_gain.reshape(-1, gain_rows),
        ],
        axis=1,
    )

    def send_rows(*after):
        return far_send(
            [hold(part, *after) for part in grad_lin.reshape(dp_count, ring_rows, width)], dp_count
        )

    def send_gains(*after):
        parts = lax.all_to_all(
            hold(gain_grads, *after), ("seq", "dp"), split_axis=0, concat_axis=0, tiled=True
        )
        return jnp.sum(parts, axis=0)

    if share:
        far_normed = jnp.concatenate(far_normed_pieces, axis=0)
        far_cot = jnp.concatenate(far_cot_pieces, axis=0)
        gate_val = by_rows(hold(far_normed, now), gate_weight)
        now = scatter_one.send(gate_val)
        row_parts = send_rows(gate_val)
        up_val = by_rows(hold(far_normed, now), up_weight)
        d_normed = scatter_one.send(up_val)
        finish = output_gradient(up_val)
        d_active = by_rows(hold(far_cot, d_normed), down_weight)
        sigmoid_val = 1.0 / (1.0 + jnp.exp(-gate_val))
        far_active = (gate_val * sigmoid_val * up_val).astype(bf16)
        far_gate, far_up = gate_grads(d_active, gate_val, up_val, sigmoid_val)
        gain_grads = send_gains(far_up)
        now = next(scatter_two)
        grad_gate = grad_gate + by_tokens(hold(far_gate, now), far_normed)
        now = scatter_two.send(grad_gate)
        out_parts = finish(grad_gate)
        grad_up = grad_up + by_tokens(hold(far_up, now, *out_parts[:1]), far_normed)
        now = scatter_two.send(grad_up)
        grad_down = grad_down + by_tokens(hold(far_active, now), far_cot)
        mlp_out = scatter_two.send(grad_down)
        out_parts = [hold(part, grad_down) for part in out_parts]
        row_parts = [hold(part, grad_down) for part in row_parts]
    else:
        grad_gate, grad_up, grad_down = (
            lax.psum(grad.astype(bf16), "dp").astype(f32) for grad in (grad_gate, grad_up, grad_down)
        )
        row_parts, gain_grads = send_rows(now), send_gains(now)
        d_normed = run_steps(scatter_one)
        out_parts = output_gradient(d_normed)()
        next(scatter_two)
        mlp_out = run_steps(scatter_two)
    result = (hidden_state + mlp_out).astype(bf16)
    inputs = token_bf.astype(f32)
    _, norm_one_back = jax.vjp(lambda v: rms_norm(v, gains[0]), inputs)
    d_input = (d_hidden + norm_one_back(d_normed)[0]).astype(bf16)
    grad_output, grad_rows = far_sum(out_parts), far_sum(row_parts)
    gain_grads = gain_grads.reshape(2, gain_rows)

    return (
        result[None],
        d_input[None],
        grad_rows[:q_rows],
        grad_rows[q_rows : q_rows + k_rows],
        grad_rows[q_rows + k_rows :],
        grad_output,
        grad_gate,
        grad_up,
        grad_down,
        gain_grads[0],
        gain_grads[1],
    )


def solution(mesh):
    in_specs = (
        P("dp", "seq", None),
        P("dp", None),
        P(("seq", "dp"), None),
        P(("seq", "dp"), None),
        P(("seq", "dp"), None),
        P(("seq", "dp"), None),
        P("seq", None),
        P("seq", None),
        P("seq", None),
        P(("seq", "dp")),
        P(("seq", "dp")),
        P("dp", "seq", None),
    )
    out_specs = (
        P("dp", "seq", None),
        P("dp", "seq", None),
        P(("seq", "dp"), None),
        P(("seq", "dp"), None),
        P(("seq", "dp"), None),
        P(("seq", "dp"), None),
        P("seq", None),
        P("seq", None),
        P("seq", None),
        P(("seq", "dp")),
        P(("seq", "dp")),
    )
    return jax.shard_map(shards, mesh=mesh, in_specs=in_specs, out_specs=out_specs, check_vma=False)
```
